128 devices in a mesh: section: 16 (over x_hi, z, core), dp: 8 (over y, x_lo).
Axes of the slice: x: 4 (x_hi: 2, x_lo: 2; x = x_hi * 2 + x_lo), y: 4, z: 4, core: 2. Of those that a mesh axis runs over, the one named last changes fastest.
Arguments:
- section_of_layer: int32 [20], replicated, may hold values from 0 to 15, as said below
- lengths: int32 [2, 2, 8], P(None, None, 'dp'), may hold values from 32 to 64, as said below
- layer_gains: float32 [20, 3, 2560], replicated, may hold values from 0.5 to 1.5
- saved_queries: bfloat16 [2, 16, 2, 2, 512, 2560], P(None, 'section', None, None, 'dp'), may hold values from -6 to 6
- saved_keys: bfloat16 [2, 16, 2, 2, 512, 2560], P(None, 'section', None, None, 'dp'), may hold values from -6 to 6
- block_inputs: bfloat16 [2, 16, 2, 512, 2560], P(None, 'section', None, 'dp'), may hold values from -400 to 400
- cotangents: bfloat16 [2, 2, 512, 2560], P(None, None, 'dp'), may hold values from -6 to 6
Outputs:
- input_grads: bfloat16 [2, 16, 2, 512, 2560], P(None, 'section', None, 'dp')
- gain_grads: float32 [16, 2, 3, 2560], P('section')
The draws below stay inside these ranges and needn't reach their ends.
Inputs may be any that keep to these rules, and one draw needn't show every extreme that they name: `section_of_layer`: never falls; every block holds 1 or 2 layers and some block holds 2; saved slots past a block's layers are unused. `lengths`: some sequence has 64 valid tokens.
All inputs are finite; a program needn't handle non-finite values.
Results may differ from the reference program's by a relative error of at most 0.012.
Values may be sent and summed in bfloat16 or wider, within the bound.
A program may use at most 128 MiB of HBM per device.

```python
import math
import jax
import jax.numpy as jnp
from jax import lax

HEADS = 20
HEAD_DIM = 128
D = 2560
SEQ = 64
MB = 2
SLOTS = 2
SECTIONS = 16
LAYERS = 20
TOKENS = 512
N_DP = 8


def draw_section_of_layer(key, part):
    shuffled = jax.random.permutation(key, SECTIONS).astype(jnp.int32)
    extra_count = LAYERS - SECTIONS
    counts = 1 + (shuffled < extra_count).astype(jnp.int32)
    block_ends = jnp.cumsum(counts).astype(jnp.int32)
    layer_ids = jnp.arange(LAYERS, dtype=jnp.int32)
    return jnp.sum((block_ends[None, :] <= layer_ids[:, None]).astype(jnp.int32), axis=1).astype(jnp.int32)


def draw_lengths(key, part):
    first_key, second_key = jax.random.split(key)
    total_count = 2 * MB * N_DP
    drawn = jax.random.randint(first_key, (total_count,), SEQ // 2, SEQ + 1, dtype=jnp.int32)
    full_spot = jax.random.randint(second_key, (), 0, total_count, dtype=jnp.int32)
    flat_lengths = jnp.where(jnp.arange(total_count, dtype=jnp.int32) == full_spot, SEQ, drawn)
    return flat_lengths.reshape(2, MB, N_DP).astype(jnp.int32)


def attention_pair(key):
    base_key = jax.random.fold_in(key, 17)
    key_list = jax.random.split(base_key, 2)
    full_shape = (2, SECTIONS, SLOTS, MB, N_DP, SEQ, HEADS, HEAD_DIM)
    query_base = jnp.clip(jax.random.normal(key_list[0], full_shape, jnp.float32), -6.0, 6.0)
    key_base = jnp.clip(jax.random.normal(key_list[1], full_shape, jnp.float32), -6.0, 6.0)
    out_shape = (2, SECTIONS, SLOTS, MB, N_DP * SEQ, HEADS * HEAD_DIM)
    return (query_base.reshape(out_shape).astype(jnp.bfloat16), key_base.reshape(out_shape).astype(jnp.bfloat16))


def draw_saved_queries(key, part):
    return attention_pair(key)[0]


def draw_saved_keys(key, part):
    return attention_pair(key)[1]


def draw_block_inputs(key, part):
    feature_count = HEADS * HEAD_DIM
    full_shape = (2, SECTIONS, MB, N_DP * SEQ, feature_count)
    key_list = jax.random.split(jax.random.fold_in(key, 29), 3)
    row_scale = jnp.exp(jax.random.uniform(key_list[1], (2, SECTIONS, MB, N_DP * SEQ, 1), jnp.float32, 0.0, math.log(10.0)))
    column_scale = jnp.exp(jax.random.uniform(key_list[2], (feature_count,), jnp.float32, 0.0, math.log(10.0)))
    core_part = jnp.clip(jax.random.normal(key_list[0], full_shape, jnp.float32), -4.0, 4.0)
    drawn = core_part * row_scale * column_scale
    return drawn.astype(jnp.bfloat16)


def block_levels(own_key, extent, shards, low, largest):
    def one(axis_at, blocks):
        steps = jax.random.uniform(jax.random.fold_in(jax.random.fold_in(own_key, 6), axis_at), (blocks,), jnp.float32, low / len(shards), largest / len(shards))
        return jnp.repeat(jnp.exp(steps), extent[axis_at] // blocks).reshape((-1,) + (1,) * (len(extent) - axis_at - 1))

    factor_of = one(*shards[0])
    for cut in shards[1:]:
        factor_of = factor_of * one(*cut)
    return factor_of


def normal_values(own_key, dims, deviation, reach, pieces=(), held_as=jnp.bfloat16):
    factor_of = block_levels(own_key, dims, pieces, -0.22, 0.18) if pieces else 1.0
    values = jax.random.normal(own_key, dims, jnp.float32) * deviation * factor_of
    return jnp.minimum(jnp.maximum(values, -reach), reach).astype(held_as)


def setup_inputs(seed: int = 0) -> dict:
    key_of = jax.random.split(jax.random.key(seed), 8)
    return {
        "section_of_layer": draw_section_of_layer(jax.random.fold_in(key_of[7], 71), 0),
        "lengths": draw_lengths(jax.random.fold_in(key_of[7], 71), 0),
        "layer_gains": jnp.clip(jax.random.uniform(key_of[2], (LAYERS, 3, D), jnp.float32, 0.5, 1.5), 0.5, 1.5),
        "saved_queries": draw_saved_queries(jax.random.fold_in(key_of[7], 71), 0),
        "saved_keys": draw_saved_keys(jax.random.fold_in(key_of[7], 71), 0),
        "block_inputs": draw_block_inputs(jax.random.fold_in(key_of[7], 71), 0),
        "cotangents": normal_values(key_of[6], (2, MB, TOKENS, D), 1.0, 6.0, ((2, 8),)),
    }


norm_epsilon = 1e-06

def split_heads(tensor):
    return tensor.reshape(tensor.shape[0], tensor.shape[1], tensor.shape[2] // HEAD_DIM, HEAD_DIM)

def merge_heads(tensor):
    return tensor.reshape(tensor.shape[0], tensor.shape[1], tensor.shape[2] * tensor.shape[3])

def product(spec, left, right):
    return jnp.einsum(spec, left.astype(jnp.float32), right.astype(jnp.float32))

def attention_mask(length, seq_len):
    rows_iota = lax.broadcasted_iota(jnp.int32, (seq_len, seq_len), 0)
    cols_iota = lax.broadcasted_iota(jnp.int32, (seq_len, seq_len), 1)
    causal = cols_iota <= rows_iota
    return causal[None, None] & (cols_iota[None, None] < length[:, None, None, None])

def layer_parts(state_in, query_in, key_in, gain_rows, length):
    seq_len = state_in.shape[1]
    score_scale = 1.0 / math.sqrt(HEAD_DIM)
    state_wide = state_in.astype(jnp.float32)
    inv_rms = lax.rsqrt(lax.optimization_barrier(jnp.mean(state_wide * state_wide, axis=-1, keepdims=True)) + norm_epsilon)
    normed = state_wide * inv_rms
    values = (normed * gain_rows[0]).astype(jnp.bfloat16)
    query_scaled = (query_in.astype(jnp.float32) * gain_rows[1]).astype(jnp.bfloat16)
    key_scaled = (key_in.astype(jnp.float32) * gain_rows[2]).astype(jnp.bfloat16)
    scores = product('gihc,gjhc->ghij', split_heads(query_scaled), split_heads(key_scaled)) * score_scale
    allowed = attention_mask(length, seq_len)
    masked = jnp.where(allowed, scores, -1e+30)
    row_top = lax.optimization_barrier(jnp.max(masked, axis=-1, keepdims=True))
    exp_terms = jnp.where(allowed, jnp.exp(masked - row_top), 0.0)
    attn_probs = exp_terms / lax.optimization_barrier(jnp.sum(exp_terms, axis=-1, keepdims=True))
    return (inv_rms, normed, values, query_scaled, key_scaled, attn_probs)

def layer_forward(state_in, parts):
    mixed_heads = product('ghij,gjhc->gihc', parts[5].astype(jnp.bfloat16), split_heads(parts[2]))
    return (state_in.astype(jnp.float32) + merge_heads(mixed_heads)).astype(jnp.bfloat16)

def layer_backward(grad_out, gain_rows, query_in, key_in, parts):
    inv_rms, normed, values, query_scaled, key_scaled, attn_probs = parts
    score_scale = 1.0 / math.sqrt(HEAD_DIM)
    grad_heads = split_heads(grad_out)
    probs_low = attn_probs.astype(jnp.bfloat16)
    value_grad = merge_heads(product('ghij,gihc->gjhc', probs_low, grad_heads))
    probs_grad = product('gihc,gjhc->ghij', grad_heads, split_heads(values))
    row_delta = lax.optimization_barrier(jnp.sum(attn_probs * probs_grad, axis=-1, keepdims=True))
    score_grad = (attn_probs * (probs_grad - row_delta) * score_scale).astype(jnp.bfloat16)
    query_grad = merge_heads(product('ghij,gjhc->gihc', score_grad, split_heads(key_scaled)))
    key_grad = merge_heads(product('ghij,gihc->gjhc', score_grad, split_heads(query_scaled)))
    gain_terms = jnp.stack([lax.optimization_barrier(jnp.sum(value_grad * normed, axis=(0, 1))), lax.optimization_barrier(jnp.sum(query_grad * query_in.astype(jnp.float32), axis=(0, 1))), lax.optimization_barrier(jnp.sum(key_grad * key_in.astype(jnp.float32), axis=(0, 1)))])
    normed_grad = value_grad * gain_rows[0]
    state_grad = inv_rms * (normed_grad - normed * lax.optimization_barrier(jnp.mean(normed_grad * normed, axis=-1, keepdims=True)))
    return ((grad_out.astype(jnp.float32) + state_grad).astype(jnp.bfloat16), gain_terms)

def block_backward(state_in, query_pair, key_pair, gain_pair, layer_count, grad_out, length):
    first_parts = layer_parts(state_in, query_pair[0], key_pair[0], gain_pair[0], length)

    def two_layers(unused):
        middle = layer_forward(state_in, first_parts)
        second = layer_parts(middle, query_pair[1], key_pair[1], gain_pair[1], length)
        inner_grad, upper_terms = layer_backward(grad_out, gain_pair[1], query_pair[1], key_pair[1], second)
        outer_grad, lower_terms = layer_backward(inner_grad, gain_pair[0], query_pair[0], key_pair[0], first_parts)
        return (outer_grad, jnp.stack([lower_terms, upper_terms]))

    def one_layer(unused):
        outer_grad, lower_terms = layer_backward(grad_out, gain_pair[0], query_pair[0], key_pair[0], first_parts)
        return (outer_grad, jnp.stack([lower_terms, jnp.zeros_like(lower_terms)]))
    return lax.cond(layer_count == 2, two_layers, one_layer, 0)

def block_layers(section_of_layer, block_index, layer_gains):
    layer_count = jnp.sum((section_of_layer == block_index).astype(jnp.int32)).astype(jnp.int32)
    first_layer = jnp.sum((section_of_layer < block_index).astype(jnp.int32)).astype(jnp.int32)
    last_layer = layer_gains.shape[0] - 1
    lower_gain = lax.dynamic_index_in_dim(layer_gains, jnp.minimum(first_layer, last_layer).astype(jnp.int32), 0, keepdims=False)
    upper_gain = lax.dynamic_index_in_dim(layer_gains, jnp.minimum(first_layer + 1, last_layer).astype(jnp.int32), 0, keepdims=False)
    return (layer_count, jnp.stack([lower_gain, upper_gain]))

def reference(section_of_layer, lengths, layer_gains, saved_queries, saved_keys, block_inputs, cotangents):
    sections = SECTIONS
    seq_len = SEQ
    groups = N_DP
    feature_count = HEADS * HEAD_DIM
    grads_total = jnp.zeros((sections, SLOTS, 3, feature_count), jnp.float32)
    positions = lax.broadcasted_iota(jnp.int32, (seq_len,), 0)
    direction_out = []
    for direction in range(2):
        micro_out = []
        for micro_index in range(MB):
            length = lengths[direction, micro_index]
            keep_rows = positions[None, :] < length[:, None]
            seed_grad = cotangents[direction, micro_index].reshape(groups, seq_len, feature_count)
            seed_grad = jnp.where(keep_rows[:, :, None], seed_grad, jnp.zeros((), jnp.bfloat16))

            def chain_step(grad_in, step_index, direction=direction, micro_index=micro_index, length=length):
                block_index = (sections - 1 - step_index).astype(jnp.int32)
                if direction == 0:
                    position = block_index
                else:
                    position = step_index.astype(jnp.int32)
                state_all = lax.dynamic_index_in_dim(block_inputs[direction], position, 0, keepdims=False)
                state_in = state_all[micro_index].reshape(groups, seq_len, feature_count)
                query_all = lax.dynamic_index_in_dim(saved_queries[direction], position, 0, keepdims=False)
                key_all = lax.dynamic_index_in_dim(saved_keys[direction], position, 0, keepdims=False)
                query_pair = query_all[:, micro_index].reshape(SLOTS, groups, seq_len, feature_count)
                key_pair = key_all[:, micro_index].reshape(SLOTS, groups, seq_len, feature_count)
                layer_count, gain_pair = block_layers(section_of_layer, block_index, layer_gains)
                grad_next, gain_terms = block_backward(state_in, query_pair, key_pair, gain_pair, layer_count, grad_in, length)
                return (grad_next, (grad_next, gain_terms))
            final_grad, (grad_seq, term_seq) = lax.scan(chain_step, seed_grad, jnp.arange(sections, dtype=jnp.int32))
            if direction == 0:
                grad_seq = grad_seq[::-1]
            micro_out.append(grad_seq.reshape(sections, groups * seq_len, feature_count))
            grads_total = grads_total + term_seq[::-1]
        direction_out.append(jnp.stack(micro_out, axis=1))
    input_grads = jnp.stack(direction_out)
    return (input_grads, grads_total / groups)
```

```python
import functools
import math

import jax
import jax.numpy as jnp
from jax import lax
from jax.experimental import pallas as pl
from jax.experimental.pallas import tpu as pltpu
from jax.sharding import PartitionSpec as P

HEAD_DIM = 128
PAIR = 2 * HEAD_DIM
EPSILON = 1e-06
MESH = pl.DeviceIdType.MESH
F32 = jnp.float32
BF16 = jnp.bfloat16


def blocks_apart(pair):
    zero = jnp.zeros((pair.shape[0], HEAD_DIM), pair.dtype)
    upper = jnp.concatenate([pair[:, :HEAD_DIM], zero], axis=1)
    lower = jnp.concatenate([zero, pair[:, HEAD_DIM:]], axis=1)
    return jnp.concatenate([upper, lower], axis=0)


def dot(left, right, left_dim, right_dim):
    return lax.dot_general(
        left, right, (((left_dim,), (right_dim,)), ((), ())), preferred_element_type=F32
    )


def kernel(
    sections,
    layers_ref,
    lengths_ref,
    gains_ref,
    queries_hbm,
    keys_hbm,
    inputs_hbm,
    cotangents_hbm,
    grads_hbm,
    terms_ref,
    q_buf,
    k_buf,
    h_buf,
    v_buf,
    p_wide,
    p_low,
    r_buf,
    e_buf,
    x_buf,
    g_buf,
    load_sems,
    seed_sems,
    op_send,
    op_recv,
    hop_send,
    hop_recv,
    set_send,
    set_recv,
    out_sems,
):
    place = lax.axis_index("section")
    core = lax.rem(place, 2)
    chip = lax.div(place, 2)
    chips = sections // 2
    seq = q_buf.shape[3]
    width = q_buf.shape[4]
    pairs = width // PAIR
    layer_total = layers_ref.shape[0]
    scale = 1.0 / math.sqrt(HEAD_DIM)
    partner = {"section": place + 1 - 2 * core}
    first_direction = jnp.where(chip >= chips // 2, 0, 1)
    leads = (chip == chips - 1) | (chip == 0)

    barrier = pltpu.get_barrier_semaphore()
    pl.semaphore_signal(barrier, inc=1, device_id=partner, device_id_type=MESH)

    @pl.when(chip > 0)
    def _():
        pl.semaphore_signal(barrier, inc=1, device_id={"section": place - 2}, device_id_type=MESH)

    @pl.when(chip < chips - 1)
    def _():
        pl.semaphore_signal(barrier, inc=1, device_id={"section": place + 2}, device_id_type=MESH)

    def loads(d, m):
        copies = [pltpu.make_async_copy(inputs_hbm.at[d, 0, m], h_buf.at[d, m, 0], load_sems.at[d, m, 0])]
        for slot in range(2):
            copies.append(
                pltpu.make_async_copy(
                    keys_hbm.at[d, 0, slot, m], k_buf.at[d, m, slot], load_sems.at[d, m, 1 + 2 * slot]
                )
            )
            copies.append(
                pltpu.make_async_copy(
                    queries_hbm.at[d, 0, slot, m], q_buf.at[d, m, slot], load_sems.at[d, m, 2 + 2 * slot]
                )
            )
        return copies

    def seed(d):
        return pltpu.make_async_copy(cotangents_hbm.at[d, core], e_buf.at[d, 0], seed_sems.at[d])

    for phase in range(2):
        d = first_direction if phase == 0 else 1 - first_direction
        for m in (1 - core, core):
            for copy in loads(d, m):
                copy.start()
        if phase == 0:

            @pl.when(leads)
            def _():
                seed(d).start()

    for d in range(2):
        for whose in range(2):
            at = place if whose == 0 else place + 1 - 2 * core
            block = at if d == 0 else sections - 1 - at
            before = jnp.int32(0)
            for layer in range(layer_total):
                before = before + jnp.where(layers_ref[layer] < block, 1, 0)
            for slot in range(2):
                layer = jnp.minimum(before + slot, layer_total - 1)
                g_buf[d, whose, slot, 0:3, :] = gains_ref[layer]

    terms_ref[...] = jnp.zeros_like(terms_ref)

    def second_layer(d):
        block = jnp.where(d == 0, place, sections - 1 - place)
        count = jnp.int32(0)
        for layer in range(layer_total):
            count = count + jnp.where(layers_ref[layer] == block, 1, 0)
        return count == 2

    neighbours = 1 + jnp.where(chip > 0, 1, 0) + jnp.where(chip < chips - 1, 1, 0)
    pl.semaphore_wait(barrier, neighbours)

    def operand_copies(d):
        mine = 1 - core
        parts = (
            (p_low.at[d, mine], p_low.at[d, 2]),
            (h_buf.at[d, mine, 0:2], h_buf.at[d, 2, 0:2]),
            (r_buf.at[d, mine], r_buf.at[d, 2]),
        )
        return [
            pltpu.make_async_remote_copy(
                src_ref=source,
                dst_ref=target,
                send_sem=op_send.at[d, at],
                recv_sem=op_recv.at[d, at],
                device_id=partner,
                device_id_type=MESH,
            )
            for at, (source, target) in enumerate(parts)
        ]

    def hop(d):
        step = jnp.where(d == 0, -2, 2)
        return pltpu.make_async_remote_copy(
            src_ref=e_buf.at[d, 4],
            dst_ref=e_buf.at[d, 0],
            send_sem=hop_send.at[d],
            recv_sem=hop_recv.at[d],
            device_id={"section": place + step},
            device_id_type=MESH,
        )

    def own_base(d):
        return jnp.where(core == 1 - d, 0, 2)

    def set_copy(d):
        return pltpu.make_async_remote_copy(
            src_ref=e_buf.at[d, pl.ds(2 - own_base(d), 3)],
            dst_ref=e_buf.at[d, 5:8],
            send_sem=set_send.at[d],
            recv_sem=set_recv.at[d],
            device_id=partner,
            device_id_type=MESH,
        )

    def out_copies(d):
        return (
            pltpu.make_async_copy(
                e_buf.at[d, own_base(d) + 2], grads_hbm.at[d, 0, core], out_sems.at[d, 0]
            ),
            pltpu.make_async_copy(e_buf.at[d, 7], grads_hbm.at[d, 0, 1 - core], out_sems.at[d, 1]),
        )

    def lane_spread(column):
        return jnp.broadcast_to(column, (seq, HEAD_DIM))

    def prepare(d):
        two = second_layer(d)

        @pl.loop(0, 2)
        def _(turn):
            m = jnp.where(turn == 0, 1 - core, core)
            for copy in loads(d, m):
                copy.wait()
            length = lengths_ref[d, m, 0]
            key_at = lax.broadcasted_iota(jnp.int32, (seq, 2 * seq), 0)
            query_at = lax.rem(lax.broadcasted_iota(jnp.int32, (seq, 2 * seq), 1), seq)
            allowed = (key_at <= query_at) & (key_at < length)

            @pl.loop(0, 2)
            def _(slot):
                squares = jnp.zeros((seq, HEAD_DIM), F32)
                for tile in range(width // HEAD_DIM):
                    part = h_buf[d, m, slot, :, tile * HEAD_DIM : (tile + 1) * HEAD_DIM].astype(F32)
                    squares = squares + part * part
                inverse = lax.rsqrt(jnp.sum(squares, axis=1, keepdims=True) * (1.0 / width) + EPSILON)
                spread = lane_spread(inverse)
                spread_two = jnp.concatenate([spread, spread], axis=1)
                present = (slot == 0) | two
                r_buf[d, m, slot] = jnp.where(present, spread, 0.0)
                for pair in range(pairs):
                    cols = slice(pair * PAIR, (pair + 1) * PAIR)
                    state = h_buf[d, m, slot, :, cols].astype(F32)
                    values = (state * spread_two * g_buf[d, 0, slot, 0:1, cols]).astype(BF16)
                    v_buf[d, m, slot, :, cols] = values
                    scaled_q = (q_buf[d, m, slot, :, cols].astype(F32) * g_buf[d, 0, slot, 1:2, cols]).astype(BF16)
                    scaled_k = (k_buf[d, m, slot, :, cols].astype(F32) * g_buf[d, 0, slot, 2:3, cols]).astype(BF16)
                    scores = dot(scaled_k, blocks_apart(scaled_q), 1, 1) * scale
                    masked = jnp.where(allowed, scores, -1e30)
                    top = jnp.max(masked, axis=0, keepdims=True)
                    terms = jnp.where(allowed, jnp.exp(masked - top), 0.0)
                    probs = terms * (1.0 / jnp.sum(terms, axis=0, keepdims=True))
                    low = probs.astype(BF16)
                    p_wide[d, m, slot, pair] = probs
                    p_low[d, m, slot, pair] = low
                    mixed = dot(low, values, 0, 0)
                    mixed = jnp.concatenate([mixed[:seq, :HEAD_DIM], mixed[seq:, HEAD_DIM:]], axis=1)
                    h_buf[d, m, slot + 1, :, cols] = (state + mixed).astype(BF16)

            @pl.when(turn == 0)
            def _():
                for copy in operand_copies(d):
                    copy.start()

    def chain(d):
        leading = jnp.where(d == 0, chip == chips - 1, chip == 0)

        @pl.when(leading)
        def _():
            seed(d).wait()
            length = lengths_ref[d, core, 0]
            rows = lax.broadcasted_iota(jnp.int32, (seq, PAIR), 0)
            for pair in range(pairs):
                cols = slice(pair * PAIR, (pair + 1) * PAIR)
                drawn = e_buf[d, 0, :, cols].astype(F32)
                e_buf[d, 0, :, cols] = jnp.where(rows < length, drawn, 0.0).astype(BF16)

        for copy in operand_copies(d):
            copy.wait_recv()

        @pl.when(jnp.logical_not(leading))
        def _():
            hop(d).wait_recv()

        @pl.loop(0, 4)
        def _(step):
            visited = lax.rem(lax.div(step, 2) + 1 - d, 2)
            slot = 1 - lax.rem(step, 2)
            entry = jnp.where(visited == core, core, 2)
            whose = jnp.where(visited == core, 0, 1)
            total = jnp.zeros((seq, HEAD_DIM), F32)
            for pair in range(pairs):
                cols = slice(pair * PAIR, (pair + 1) * PAIR)
                grad = e_buf[d, step, :, cols]
                product = dot(p_low[d, entry, slot, pair], blocks_apart(grad), 1, 0)
                product = product * g_buf[d, whose, slot, 0:1, cols]
                x_buf[:, cols] = product
                weighed = product * h_buf[d, entry, slot, :, cols].astype(F32)
                total = total + (weighed[:, :HEAD_DIM] + weighed[:, HEAD_DIM:])
            inverse = r_buf[d, entry, slot]
            shift = lane_spread(jnp.sum(total, axis=1, keepdims=True) * (1.0 / width))
            shift = shift * inverse * inverse * inverse
            for tile in range(width // HEAD_DIM):
                cols = slice(tile * HEAD_DIM, (tile + 1) * HEAD_DIM)
                state = h_buf[d, entry, slot, :, cols].astype(F32)
                grad = e_buf[d, step, :, cols].astype(F32)
                e_buf[d, step + 1, :, cols] = (grad + (inverse * x_buf[:, cols] - state * shift)).astype(BF16)

        ending = jnp.where(d == 0, chip == 0, chip == chips - 1)

        @pl.when(jnp.logical_not(ending))
        def _():
            hop(d).start()

        set_copy(d).start()
        out_copies(d)[0].start()

    def gain_terms(d):
        two = second_layer(d)

        @pl.loop(0, 2)
        def _(turn):
            m = jnp.where(turn == 0, core, 1 - core)
            base = jnp.where(turn == 0, own_base(d), 5)

            @pl.when(turn == 1)
            def _():
                set_copy(d).wait_recv()
                out_copies(d)[1].start()

            @pl.loop(0, 2)
            def _(slot):
                at = base + 1 - slot
                inverse = r_buf[d, m, slot]
                inverse_two = jnp.concatenate([inverse, inverse], axis=1)
                for pair in range(pairs):
                    cols = slice(pair * PAIR, (pair + 1) * PAIR)
                    grad = blocks_apart(e_buf[d, at, :, cols])
                    value_grad = dot(p_low[d, m, slot, pair], grad, 1, 0)
                    normed = h_buf[d, m, slot, :, cols].astype(F32) * inverse_two
                    norm_term = jnp.sum(value_grad * normed, axis=0, keepdims=True)
                    probs_grad = dot(v_buf[d, m, slot, :, cols], grad, 1, 1)
                    probs = p_wide[d, m, slot, pair]
                    delta = jnp.sum(probs * probs_grad, axis=0, keepdims=True)
                    score_grad = (probs * (probs_grad - delta) * scale).astype(BF16)
                    met = dot(score_grad, blocks_apart(q_buf[d, m, slot, :, cols]), 1, 0)
                    shared = jnp.sum(met * k_buf[d, m, slot, :, cols].astype(F32), axis=0, keepdims=True)
                    shared = jnp.where((slot == 0) | two, shared, 0.0)
                    terms_ref[d, slot, 0:1, cols] += norm_term
                    terms_ref[d, slot, 1:2, cols] += shared * g_buf[d, 0, slot, 2:3, cols]
                    terms_ref[d, slot, 2:3, cols] += shared * g_buf[d, 0, slot, 1:2, cols]

    early = leads & (core == 0)

    @pl.loop(0, 6)
    def _(t):
        chain_first = jnp.where(early, 1, 2)
        is_chain = (t == chain_first) | (t == 4)
        is_terms = (t == 3) | (t == 5)
        late = (t >= 4) | ((t >= 1) & (t <= 2) & (t != chain_first))
        d = jnp.where(late, 1 - first_direction, first_direction)

        @pl.when(is_chain)
        def _():
            chain(d)

        @pl.when(is_terms)
        def _():
            gain_terms(d)

        @pl.when(jnp.logical_not(is_chain | is_terms))
        def _():
            prepare(d)

    for d in range(2):
        for copy in operand_copies(d):
            copy.wait_send()
        set_copy(d).wait_send()
        for copy in out_copies(d):
            copy.wait()
        ending = (chip == 0) if d == 0 else (chip == chips - 1)

        @pl.when(jnp.logical_not(ending))
        def _():
            hop(d).wait_send()


def body(
    section_of_layer, lengths, layer_gains, saved_queries, saved_keys, block_inputs, cotangents
):
    sections = lax.axis_size("section")
    groups = lax.axis_size("dp")
    seq, width = block_inputs.shape[3:]
    pairs = width // PAIR
    anywhere = pl.BlockSpec(memory_space=pl.ANY)
    scalars = pl.BlockSpec(memory_space=pltpu.SMEM)
    vector = pl.BlockSpec(memory_space=pltpu.VMEM)
    dma = pltpu.SemaphoreType.DMA
    input_grads, terms = pl.pallas_call(
        functools.partial(kernel, sections),
        out_shape=(
            jax.ShapeDtypeStruct(block_inputs.shape, BF16),
            jax.ShapeDtypeStruct((2, 2, 8, width), F32),
        ),
        in_specs=[scalars, scalars, vector, anywhere, anywhere, anywhere, anywhere],
        out_specs=(anywhere, vector),
        scratch_shapes=[
            pltpu.VMEM((2, 2, 2, seq, width), BF16),
            pltpu.VMEM((2, 2, 2, seq, width), BF16),
            pltpu.VMEM((2, 3, 3, seq, width), BF16),
            pltpu.VMEM((2, 2, 2, seq, width), BF16),
            pltpu.VMEM((2, 2, 2, pairs, seq, 2 * seq), F32),
            pltpu.VMEM((2, 3, 2, pairs, seq, 2 * seq), BF16),
            pltpu.VMEM((2, 3, 2, seq, HEAD_DIM), F32),
            pltpu.VMEM((2, 8, seq, width), BF16),
            pltpu.VMEM((seq, width), F32),
            pltpu.VMEM((2, 2, 2, 8, width), F32),
            dma((2, 2, 5)),
            dma((2,)),
            dma((2, 3)),
            dma((2, 3)),
            dma((2,)),
            dma((2,)),
            dma((2,)),
            dma((2,)),
            dma((2, 2)),
        ],
        compiler_params=pltpu.CompilerParams(
            collective_id=0, has_side_effects=True, vmem_limit_bytes=60000 * 1024
        ),
    )(section_of_layer, lengths, layer_gains, saved_queries, saved_keys, block_inputs, cotangents)
    mirrored = lax.ppermute(
        terms[1], "section", [(at, sections - 1 - at) for at in range(sections)]
    )
    own_rows = lax.psum(terms[0] + mirrored, "dp")
    gain_grads = (own_rows[:, 0:3] / groups)[None]
    return (input_grads, gain_grads)


def solution(mesh):
    in_specs = (
        P(),
        P(None, None, "dp"),
        P(),
        P(None, "section", None, None, "dp", None),
        P(None, "section", None, None, "dp", None),
        P(None, "section", None, "dp", None),
        P(None, None, "dp", None),
    )
    out_specs = (P(None, "section", None, "dp", None), P("section", None, None, None))
    return jax.shard_map(body, mesh=mesh, in_specs=in_specs, out_specs=out_specs, check_vma=False)
```

```python
import functools
import math

import jax
import jax.numpy as jnp
from jax import lax
from jax.experimental import pallas as pl
from jax.experimental.pallas import tpu as pltpu
from jax.sharding import PartitionSpec as P

HEAD_DIM = 128
PAIR = 2 * HEAD_DIM
EPSILON = 1e-06
MESH = pl.DeviceIdType.MESH
F32 = jnp.float32
BF16 = jnp.bfloat16


def blocks_apart(pair):
    zero = jnp.zeros((pair.shape[0], HEAD_DIM), pair.dtype)
    upper = jnp.concatenate([pair[:, :HEAD_DIM], zero], axis=1)
    lower = jnp.concatenate([zero, pair[:, HEAD_DIM:]], axis=1)
    return jnp.concatenate([upper, lower], axis=0)


def dot(left, right, left_dim, right_dim):
    return lax.dot_general(
        left, right, (((left_dim,), (right_dim,)), ((), ())), preferred_element_type=F32
    )


def kernel(
    sections,
    layers_ref,
    lengths_ref,
    gains_hbm,
    queries_hbm,
    keys_hbm,
    inputs_hbm,
    cotangents_hbm,
    grads_hbm,
    sums_ref,
    gains_ref,
    terms_ref,
    sent_terms,
    met_terms,
    final_terms,
    q_buf,
    k_buf,
    h_buf,
    v_buf,
    p_wide,
    p_low,
    r_buf,
    e_buf,
    x_buf,
    g_buf,
    load_sems,
    seed_sems,
    op_send,
    op_recv,
    hop_send,
    hop_recv,
    set_send,
    set_recv,
    out_sems,
    gain_sem,
    scatter_send,
    scatter_recv,
    gather_send,
    gather_recv,
):
    place = lax.axis_index("section")
    group = lax.axis_index("dp")
    groups = scatter_recv.shape[1]
    reducers = gather_recv.shape[0]
    core = lax.rem(place, 2)
    chip = lax.div(place, 2)
    chips = sections // 2
    seq = q_buf.shape[3]
    width = q_buf.shape[4]
    pairs = width // PAIR
    layer_total = layers_ref.shape[0]
    chunk = width // reducers
    scale = 1.0 / math.sqrt(HEAD_DIM)
    partner = {"section": place + 1 - 2 * core}
    first_direction = jnp.where(chip >= chips // 2, 0, 1)
    leads = (chip == chips - 1) | (chip == 0)

    barrier = pltpu.get_barrier_semaphore()
    pl.semaphore_signal(barrier, inc=1, device_id=partner, device_id_type=MESH)

    @pl.when(chip > 0)
    def _():
        pl.semaphore_signal(barrier, inc=1, device_id={"section": place - 2}, device_id_type=MESH)

    @pl.when(chip < chips - 1)
    def _():
        pl.semaphore_signal(barrier, inc=1, device_id={"section": place + 2}, device_id_type=MESH)

    for other in range(groups):

        @pl.when(other != group)
        def _():
            pl.semaphore_signal(barrier, inc=1, device_id={"dp": jnp.int32(other)}, device_id_type=MESH)

        pl.semaphore_signal(
            barrier,
            inc=1,
            device_id={"section": sections - 1 - place, "dp": jnp.int32(other)},
            device_id_type=MESH,
        )

    gain_load = pltpu.make_async_copy(gains_hbm, gains_ref, gain_sem)
    gain_load.start()

    def loads(d, m):
        copies = [pltpu.make_async_copy(inputs_hbm.at[d, 0, m], h_buf.at[d, m, 0], load_sems.at[d, m, 0])]
        for slot in range(2):
            copies.append(
                pltpu.make_async_copy(
                    keys_hbm.at[d, 0, slot, m], k_buf.at[d, m, slot], load_sems.at[d, m, 1 + 2 * slot]
                )
            )
            copies.append(
                pltpu.make_async_copy(
                    queries_hbm.at[d, 0, slot, m], q_buf.at[d, m, slot], load_sems.at[d, m, 2 + 2 * slot]
                )
            )
        return copies

    def seed(d):
        return pltpu.make_async_copy(cotangents_hbm.at[d, core], e_buf.at[d, 0], seed_sems.at[d])

    for phase in range(2):
        d = first_direction if phase == 0 else 1 - first_direction
        for m in (1 - core, core):
            for copy in loads(d, m):
                copy.start()
        if phase == 0:

            @pl.when(leads)
            def _():
                seed(d).start()

    gain_load.wait()

    for d in range(2):
        for whose in range(2):
            at = place if whose == 0 else place + 1 - 2 * core
            block = at if d == 0 else sections - 1 - at
            before = jnp.int32(0)
            for layer in range(layer_total):
                before = before + jnp.where(layers_ref[layer] < block, 1, 0)
            for slot in range(2):
                layer = jnp.minimum(before + slot, layer_total - 1)
                for row in range(3):
                    g_buf[d, whose, slot, row : row + 1, :] = gains_ref[row, pl.ds(layer, 1), :]

    terms_ref[...] = jnp.zeros_like(terms_ref)
    sent_terms[...] = jnp.zeros_like(sent_terms)
    met_terms[0, group] = jnp.zeros((8, chunk), F32)

    def second_layer(d):
        block = jnp.where(d == 0, place, sections - 1 - place)
        count = jnp.int32(0)
        for layer in range(layer_total):
            count = count + jnp.where(layers_ref[layer] == block, 1, 0)
        return count == 2

    neighbours = 1 + jnp.where(chip > 0, 1, 0) + jnp.where(chip < chips - 1, 1, 0)
    neighbours = neighbours + 2 * groups - 1

    def operand_copies(d):
        mine = 1 - core
        parts = (
            (p_low.at[d, mine], p_low.at[d, 2]),
            (h_buf.at[d, mine, 0:2], h_buf.at[d, 2, 0:2]),
            (r_buf.at[d, mine], r_buf.at[d, 2]),
        )
        return [
            pltpu.make_async_remote_copy(
                src_ref=source,
                dst_ref=target,
                send_sem=op_send.at[d, at],
                recv_sem=op_recv.at[d, at],
                device_id=partner,
                device_id_type=MESH,
            )
            for at, (source, target) in enumerate(parts)
        ]

    def hop(d):
        step = jnp.where(d == 0, -2, 2)
        return pltpu.make_async_remote_copy(
            src_ref=e_buf.at[d, 4],
            dst_ref=e_buf.at[d, 0],
            send_sem=hop_send.at[d],
            recv_sem=hop_recv.at[d],
            device_id={"section": place + step},
            device_id_type=MESH,
        )

    def own_base(d):
        return jnp.where(core == 1 - d, 0, 2)

    def set_copy(d):
        return pltpu.make_async_remote_copy(
            src_ref=e_buf.at[d, pl.ds(2 - own_base(d), 3)],
            dst_ref=e_buf.at[d, 5:8],
            send_sem=set_send.at[d],
            recv_sem=set_recv.at[d],
            device_id=partner,
            device_id_type=MESH,
        )

    def out_copies(d):
        return (
            pltpu.make_async_copy(
                e_buf.at[d, own_base(d) + 2], grads_hbm.at[d, 0, core], out_sems.at[d, 0]
            ),
            pltpu.make_async_copy(e_buf.at[d, 7], grads_hbm.at[d, 0, 1 - core], out_sems.at[d, 1]),
        )

    def lane_spread(column):
        return jnp.broadcast_to(column, (seq, HEAD_DIM))

    def prepare(d, t):
        two = second_layer(d)

        @pl.loop(0, 2)
        def _(turn):
            m = jnp.where(turn == 0, 1 - core, core)
            for copy in loads(d, m):
                copy.wait()
            length = lengths_ref[d, 0, m]
            key_at = lax.broadcasted_iota(jnp.int32, (seq, 2 * seq), 0)
            query_at = lax.rem(lax.broadcasted_iota(jnp.int32, (seq, 2 * seq), 1), seq)
            allowed = (key_at <= query_at) & (key_at < length)

            @pl.loop(0, 2)
            def _(slot):
                squares = jnp.zeros((seq, HEAD_DIM), F32)
                for tile in range(width // HEAD_DIM):
                    part = h_buf[d, m, slot, :, tile * HEAD_DIM : (tile + 1) * HEAD_DIM].astype(F32)
                    squares = squares + part * part
                inverse = lax.rsqrt(jnp.sum(squares, axis=1, keepdims=True) * (1.0 / width) + EPSILON)
                spread = lane_spread(inverse)
                spread_two = jnp.concatenate([spread, spread], axis=1)
                present = (slot == 0) | two
                r_buf[d, m, slot] = jnp.where(present, spread, 0.0)
                for pair in range(pairs):
                    cols = slice(pair * PAIR, (pair + 1) * PAIR)
                    state = h_buf[d, m, slot, :, cols].astype(F32)
                    values = (state * spread_two * g_buf[d, 0, slot, 0:1, cols]).astype(BF16)
                    v_buf[d, m, slot, :, cols] = values
                    scaled_q = (q_buf[d, m, slot, :, cols].astype(F32) * g_buf[d, 0, slot, 1:2, cols]).astype(BF16)
                    scaled_k = (k_buf[d, m, slot, :, cols].astype(F32) * g_buf[d, 0, slot, 2:3, cols]).astype(BF16)
                    scores = dot(scaled_k, blocks_apart(scaled_q), 1, 1) * scale
                    masked = jnp.where(allowed, scores, -1e30)
                    top = jnp.max(masked, axis=0, keepdims=True)
                    terms = jnp.where(allowed, jnp.exp(masked - top), 0.0)
                    probs = terms * (1.0 / jnp.sum(terms, axis=0, keepdims=True))
                    low = probs.astype(BF16)
                    p_wide[d, m, slot, pair] = probs
                    p_low[d, m, slot, pair] = low
                    mixed = dot(low, values, 0, 0)
                    mixed = jnp.concatenate([mixed[:seq, :HEAD_DIM], mixed[seq:, HEAD_DIM:]], axis=1)
                    h_buf[d, m, slot + 1, :, cols] = (state + mixed).astype(BF16)

            @pl.when((turn == 0) & (t == 0))
            def _():
                pl.semaphore_wait(barrier, neighbours)

            @pl.when(turn == 0)
            def _():
                for copy in operand_copies(d):
                    copy.start()

    def chain(d):
        leading = jnp.where(d == 0, chip == chips - 1, chip == 0)

        @pl.when(leading)
        def _():
            seed(d).wait()
            length = lengths_ref[d, 0, core]
            rows = lax.broadcasted_iota(jnp.int32, (seq, PAIR), 0)
            for pair in range(pairs):
                cols = slice(pair * PAIR, (pair + 1) * PAIR)
                drawn = e_buf[d, 0, :, cols].astype(F32)
                e_buf[d, 0, :, cols] = jnp.where(rows < length, drawn, 0.0).astype(BF16)

        for copy in operand_copies(d):
            copy.wait_recv()

        @pl.when(jnp.logical_not(leading))
        def _():
            hop(d).wait_recv()

        @pl.loop(0, 4)
        def _(step):
            visited = lax.rem(lax.div(step, 2) + 1 - d, 2)
            slot = 1 - lax.rem(step, 2)
            entry = jnp.where(visited == core, core, 2)
            whose = jnp.where(visited == core, 0, 1)
            total = jnp.zeros((seq, HEAD_DIM), F32)
            for pair in range(pairs):
                cols = slice(pair * PAIR, (pair + 1) * PAIR)
                grad = e_buf[d, step, :, cols]
                product = dot(p_low[d, entry, slot, pair], blocks_apart(grad), 1, 0)
                product = product * g_buf[d, whose, slot, 0:1, cols]
                x_buf[:, cols] = product
                weighed = product * h_buf[d, entry, slot, :, cols].astype(F32)
                total = total + (weighed[:, :HEAD_DIM] + weighed[:, HEAD_DIM:])
            inverse = r_buf[d, entry, slot]
            shift = lane_spread(jnp.sum(total, axis=1, keepdims=True) * (1.0 / width))
            shift = shift * inverse * inverse * inverse
            for tile in range(width // HEAD_DIM):
                cols = slice(tile * HEAD_DIM, (tile + 1) * HEAD_DIM)
                state = h_buf[d, entry, slot, :, cols].astype(F32)
                grad = e_buf[d, step, :, cols].astype(F32)
                e_buf[d, step + 1, :, cols] = (grad + (inverse * x_buf[:, cols] - state * shift)).astype(BF16)

        ending = jnp.where(d == 0, chip == 0, chip == chips - 1)

        @pl.when(jnp.logical_not(ending))
        def _():
            hop(d).start()

        set_copy(d).start()
        out_copies(d)[0].start()

    def gain_terms(d):
        two = second_layer(d)

        @pl.loop(0, 2)
        def _(turn):
            m = jnp.where(turn == 0, core, 1 - core)
            base = jnp.where(turn == 0, own_base(d), 5)

            @pl.when(turn == 1)
            def _():
                set_copy(d).wait_recv()
                out_copies(d)[1].start()

            @pl.loop(0, 2)
            def _(slot):
                at = base + 1 - slot
                inverse = r_buf[d, m, slot]
                inverse_two = jnp.concatenate([inverse, inverse], axis=1)
                for pair in range(pairs):
                    cols = slice(pair * PAIR, (pair + 1) * PAIR)
                    grad = blocks_apart(e_buf[d, at, :, cols])
                    value_grad = dot(p_low[d, m, slot, pair], grad, 1, 0)
                    normed = h_buf[d, m, slot, :, cols].astype(F32) * inverse_two
                    norm_term = jnp.sum(value_grad * normed, axis=0, keepdims=True)
                    probs_grad = dot(v_buf[d, m, slot, :, cols], grad, 1, 1)
                    probs = p_wide[d, m, slot, pair]
                    delta = jnp.sum(probs * probs_grad, axis=0, keepdims=True)
                    score_grad = (probs * (probs_grad - delta) * scale).astype(BF16)
                    met = dot(score_grad, blocks_apart(q_buf[d, m, slot, :, cols]), 1, 0)
                    shared = jnp.sum(met * k_buf[d, m, slot, :, cols].astype(F32), axis=0, keepdims=True)
                    shared = jnp.where((slot == 0) | two, shared, 0.0)
                    terms_ref[d, slot, 0:1, cols] += norm_term
                    terms_ref[d, slot, 1:2, cols] += shared * g_buf[d, 0, slot, 2:3, cols]
                    terms_ref[d, slot, 2:3, cols] += shared * g_buf[d, 0, slot, 1:2, cols]

    def scatter_copy(d, reducer, source):
        target = jnp.where(d == 0, place, sections - 1 - place)
        return pltpu.make_async_remote_copy(
            src_ref=sent_terms.at[d, :, reducer * chunk : (reducer + 1) * chunk],
            dst_ref=met_terms.at[d, source],
            send_sem=scatter_send.at[d, reducer],
            recv_sem=scatter_recv.at[d, source],
            device_id={"section": target, "dp": jnp.int32(reducer)},
            device_id_type=MESH,
        )

    def gather_copy(reducer, target):
        return pltpu.make_async_remote_copy(
            src_ref=final_terms.at[reducer],
            dst_ref=final_terms.at[reducer],
            send_sem=gather_send.at[target],
            recv_sem=gather_recv.at[reducer],
            device_id={"dp": jnp.int32(target)},
            device_id_type=MESH,
        )

    def scatter(d):
        for slot in range(2):
            for row in range(3):
                at = 3 * slot + row
                sent_terms[d, at : at + 1, :] = terms_ref[d, slot, row : row + 1, :]
        for reducer in range(reducers):

            @pl.when((d == 1) | (reducer != group))
            def _():
                scatter_copy(d, reducer, group).start()

    early = leads & (core == 0)

    @pl.loop(0, 6)
    def _(t):
        chain_first = jnp.where(early, 1, 2)
        is_chain = (t == chain_first) | (t == 4)
        is_terms = (t == 3) | (t == 5)
        late = (t >= 4) | ((t >= 1) & (t <= 2) & (t != chain_first))
        d = jnp.where(late, 1 - first_direction, first_direction)

        @pl.when(jnp.logical_not(is_chain | is_terms))
        def _():
            prepare(d, t)

        @pl.when(is_chain)
        def _():
            chain(d)

        @pl.when(is_terms)
        def _():
            gain_terms(d)
            scatter(d)

    @pl.when(group < reducers)
    def _():
        total = sent_terms[0, :, pl.ds(pl.multiple_of(group * chunk, chunk), chunk)]
        for other in range(groups):
            scatter_copy(1, 0, other).wait_recv()
            total = total + met_terms[1, other]
        for other in range(groups):

            @pl.when(other != group)
            def _():
                scatter_copy(0, 0, other).wait_recv()

        for other in range(groups):
            total = total + jnp.where(other == group, 0.0, met_terms[0, other])
        final_terms[group] = total * (1.0 / groups)
        for other in range(groups):

            @pl.when(other != group)
            def _():
                gather_copy(group, other).start()

    for reducer in range(reducers):

        @pl.when(reducer != group)
        def _():
            gather_copy(reducer, 0).wait_recv()

        for slot in range(2):
            for row in range(3):
                sums_ref[0, row, slot : slot + 1, reducer * chunk : (reducer + 1) * chunk] = final_terms[
                    reducer, 3 * slot + row : 3 * slot + row + 1, :
                ]

    for other in range(groups):

        @pl.when((group < reducers) & (other != group))
        def _():
            gather_copy(group, other).wait_send()

    for reducer in range(reducers):
        scatter_copy(1, reducer, group).wait_send()

        @pl.when(reducer != group)
        def _():
            scatter_copy(0, reducer, group).wait_send()

    for d in range(2):
        for copy in operand_copies(d):
            copy.wait_send()
        set_copy(d).wait_send()
        for copy in out_copies(d):
            copy.wait()
        ending = (chip == 0) if d == 0 else (chip == chips - 1)

        @pl.when(jnp.logical_not(ending))
        def _():
            hop(d).wait_send()


def body(
    section_of_layer, lengths, layer_gains, saved_queries, saved_keys, block_inputs, cotangents
):
    sections = lax.axis_size("section")
    groups = lax.axis_size("dp")
    seq, width = block_inputs.shape[3:]
    pairs = width // PAIR
    anywhere = pl.BlockSpec(memory_space=pl.ANY)
    scalars = pl.BlockSpec(memory_space=pltpu.SMEM)
    vector = pl.BlockSpec(memory_space=pltpu.VMEM)
    dma = pltpu.SemaphoreType.DMA
    reducers = 5
    input_grads, sums = pl.pallas_call(
        functools.partial(kernel, sections),
        out_shape=(
            jax.ShapeDtypeStruct(block_inputs.shape, BF16),
            jax.ShapeDtypeStruct((1, 3, 2, width), F32),
        ),
        in_specs=[scalars, scalars, anywhere, anywhere, anywhere, anywhere, anywhere],
        out_specs=(anywhere, vector),
        scratch_shapes=[
            pltpu.VMEM((3, layer_gains.shape[0], width), F32),
            pltpu.VMEM((2, 2, 8, width), F32),
            pltpu.VMEM((2, 8, width), F32),
            pltpu.VMEM((2, groups, 8, width // reducers), F32),
            pltpu.VMEM((reducers, 8, width // reducers), F32),
            pltpu.VMEM((2, 2, 2, seq, width), BF16),
            pltpu.VMEM((2, 2, 2, seq, width), BF16),
            pltpu.VMEM((2, 3, 3, seq, width), BF16),
            pltpu.VMEM((2, 2, 2, seq, width), BF16),
            pltpu.VMEM((2, 2, 2, pairs, seq, 2 * seq), F32),
            pltpu.VMEM((2, 3, 2, pairs, seq, 2 * seq), BF16),
            pltpu.VMEM((2, 3, 2, seq, HEAD_DIM), F32),
            pltpu.VMEM((2, 8, seq, width), BF16),
            pltpu.VMEM((seq, width), F32),
            pltpu.VMEM((2, 2, 2, 8, width), F32),
            dma((2, 2, 5)),
            dma((2,)),
            dma((2, 3)),
            dma((2, 3)),
            dma((2,)),
            dma((2,)),
            dma((2,)),
            dma((2,)),
            dma((2, 2)),
            dma,
            dma((2, reducers)),
            dma((2, groups)),
            dma((groups,)),
            dma((reducers,)),
        ],
        compiler_params=pltpu.CompilerParams(
            collective_id=0, has_side_effects=True, vmem_limit_bytes=60000 * 1024
        ),
    )(
        section_of_layer,
        jnp.transpose(lengths, (0, 2, 1)),
        jnp.transpose(layer_gains, (1, 0, 2)),
        saved_queries,
        saved_keys,
        block_inputs,
        cotangents,
    )
    return (input_grads, jnp.transpose(sums, (0, 2, 1, 3)))


def solution(mesh):
    in_specs = (
        P(),
        P(None, None, "dp"),
        P(),
        P(None, "section", None, None, "dp", None),
        P(None, "section", None, None, "dp", None),
        P(None, "section", None, "dp", None),
        P(None, None, "dp", None),
    )
    out_specs = (P(None, "section", None, "dp", None), P("section", None, None, None))
    return jax.shard_map(body, mesh=mesh, in_specs=in_specs, out_specs=out_specs, check_vma=False)
```

```python
import functools
import math

import jax
import jax.numpy as jnp
from jax import lax
from jax.experimental import pallas as pl
from jax.experimental.pallas import tpu as pltpu
from jax.sharding import PartitionSpec as P

HEAD_DIM = 128
PAIR = 2 * HEAD_DIM
EPSILON = 1e-06
MESH = pl.DeviceIdType.MESH
F32 = jnp.float32
BF16 = jnp.bfloat16


def blocks_apart(pair):
    zero = jnp.zeros((pair.shape[0], HEAD_DIM), pair.dtype)
    upper = jnp.concatenate([pair[:, :HEAD_DIM], zero], axis=1)
    lower = jnp.concatenate([zero, pair[:, HEAD_DIM:]], axis=1)
    return jnp.concatenate([upper, lower], axis=0)


def dot(left, right, left_dim, right_dim):
    return lax.dot_general(
        left, right, (((left_dim,), (right_dim,)), ((), ())), preferred_element_type=F32
    )


def kernel(
    sections,
    layers_ref,
    lengths_ref,
    gains_hbm,
    queries_hbm,
    keys_hbm,
    inputs_hbm,
    cotangents_hbm,
    grads_hbm,
    sums_ref,
    gains_ref,
    terms_ref,
    sent_terms,
    met_terms,
    final_terms,
    q_buf,
    k_buf,
    h_buf,
    v_buf,
    p_wide,
    p_low,
    r_buf,
    e_buf,
    x_buf,
    g_buf,
    load_sems,
    seed_sems,
    op_send,
    op_recv,
    hop_send,
    hop_recv,
    set_send,
    set_recv,
    out_sems,
    gain_sem,
    scatter_send,
    scatter_recv,
    gather_send,
    gather_recv,
):
    place = lax.axis_index("section")
    group = lax.axis_index("dp")
    groups = scatter_recv.shape[1]
    reducers = gather_recv.shape[0]
    core = lax.rem(place, 2)
    chip = lax.div(place, 2)
    chips = sections // 2
    seq = q_buf.shape[3]
    width = q_buf.shape[4]
    pairs = width // PAIR
    layer_total = layers_ref.shape[0]
    chunk = width // reducers
    scale = 1.0 / math.sqrt(HEAD_DIM)
    partner = {"section": place + 1 - 2 * core}
    first_direction = jnp.where(chip >= chips // 2, 0, 1)
    leads = (chip == chips - 1) | (chip == 0)

    runner = core == 1
    barrier = pltpu.get_barrier_semaphore()
    pl.semaphore_signal(barrier, inc=1, device_id=partner, device_id_type=MESH)

    @pl.when(runner & (chip > 0))
    def _():
        pl.semaphore_signal(barrier, inc=1, device_id={"section": place - 2}, device_id_type=MESH)

    @pl.when(runner & (chip < chips - 1))
    def _():
        pl.semaphore_signal(barrier, inc=1, device_id={"section": place + 2}, device_id_type=MESH)

    for other in range(groups):

        @pl.when(other != group)
        def _():
            pl.semaphore_signal(barrier, inc=1, device_id={"dp": jnp.int32(other)}, device_id_type=MESH)

        pl.semaphore_signal(
            barrier,
            inc=1,
            device_id={"section": sections - 1 - place, "dp": jnp.int32(other)},
            device_id_type=MESH,
        )

    gain_load = pltpu.make_async_copy(gains_hbm, gains_ref, gain_sem)
    gain_load.start()

    def state_load(d, m):
        return pltpu.make_async_copy(inputs_hbm.at[d, 0, m], h_buf.at[d, m, 0, 0], load_sems.at[d, m, 0])

    def head_loads(d, m, slot):
        return (
            pltpu.make_async_copy(
                keys_hbm.at[d, 0, slot, m], k_buf.at[d, m, slot], load_sems.at[d, m, 1 + 2 * slot]
            ),
            pltpu.make_async_copy(
                queries_hbm.at[d, 0, slot, m], q_buf.at[d, m, slot], load_sems.at[d, m, 2 + 2 * slot]
            ),
        )

    def seed(d, m):
        return pltpu.make_async_copy(cotangents_hbm.at[d, m], e_buf.at[d, m, 0], seed_sems.at[d, m])

    for phase in range(2):
        d = first_direction if phase == 0 else 1 - first_direction
        for m in range(2):
            state_load(d, m).start()
            for slot in range(2):
                for copy in head_loads(d, m, slot):
                    copy.start()
            if phase == 0:

                @pl.when(leads & runner)
                def _():
                    seed(d, m).start()

    gain_load.wait()

    for d in range(2):
        for whose in range(2):
            at = place if whose == 0 else place + 1 - 2 * core
            block = at if d == 0 else sections - 1 - at
            before = jnp.int32(0)
            for layer in range(layer_total):
                before = before + jnp.where(layers_ref[layer] < block, 1, 0)
            for slot in range(2):
                layer = jnp.minimum(before + slot, layer_total - 1)
                for row in range(3):
                    g_buf[d, whose, slot, row : row + 1, :] = gains_ref[row, pl.ds(layer, 1), :]

    terms_ref[...] = jnp.zeros_like(terms_ref)
    sent_terms[...] = jnp.zeros_like(sent_terms)
    met_terms[0, group] = jnp.zeros((8, chunk), F32)

    def second_layer(d):
        block = jnp.where(d == 0, place, sections - 1 - place)
        count = jnp.int32(0)
        for layer in range(layer_total):
            count = count + jnp.where(layers_ref[layer] == block, 1, 0)
        return count == 2

    neighbours = 1 + core * (jnp.where(chip > 0, 1, 0) + jnp.where(chip < chips - 1, 1, 0))
    neighbours = neighbours + 2 * groups - 1

    def operand_copies(d, m):
        pieces = (
            (p_low.at[d, m, 0], p_low.at[d, m, 1]),
            (h_buf.at[d, m, 0, 0:2], h_buf.at[d, m, 1, 0:2]),
            (r_buf.at[d, m, 0], r_buf.at[d, m, 1]),
        )
        return [
            pltpu.make_async_remote_copy(
                src_ref=source,
                dst_ref=target,
                send_sem=op_send.at[d, m, at],
                recv_sem=op_recv.at[d, m, at],
                device_id=partner,
                device_id_type=MESH,
            )
            for at, (source, target) in enumerate(pieces)
        ]

    def hop(d, m):
        step = jnp.where(d == 0, -2, 2)
        return pltpu.make_async_remote_copy(
            src_ref=e_buf.at[d, m, 4],
            dst_ref=e_buf.at[d, m, 0],
            send_sem=hop_send.at[d, m],
            recv_sem=hop_recv.at[d, m],
            device_id={"section": place + step},
            device_id_type=MESH,
        )

    def stage_copy(d, m, at):
        return pltpu.make_async_remote_copy(
            src_ref=e_buf.at[d, m, 2 - 2 * d + at],
            dst_ref=e_buf.at[d, m, at],
            send_sem=set_send.at[d, m, at],
            recv_sem=set_recv.at[d, m, at],
            device_id=partner,
            device_id_type=MESH,
        )

    def own_base(d):
        return core * 2 * d

    def out_copy(d, m):
        return pltpu.make_async_copy(e_buf.at[d, m, own_base(d) + 2], grads_hbm.at[d, 0, m], out_sems.at[d, m])

    def lane_spread(column):
        return jnp.broadcast_to(column, (seq, HEAD_DIM))

    def prepare(d, m, t):
        two = second_layer(d)
        state_load(d, m).wait()
        length = lengths_ref[d, 0, m]
        key_at = lax.broadcasted_iota(jnp.int32, (seq, 2 * seq), 0)
        query_at = lax.rem(lax.broadcasted_iota(jnp.int32, (seq, 2 * seq), 1), seq)
        allowed = (key_at <= query_at) & (key_at < length)

        @pl.loop(0, 2)
        def _(slot):
            for copy in head_loads(d, m, slot):
                copy.wait()
            squares = jnp.zeros((seq, HEAD_DIM), F32)
            for tile in range(width // HEAD_DIM):
                part = h_buf[d, m, 0, slot, :, tile * HEAD_DIM : (tile + 1) * HEAD_DIM].astype(F32)
                squares = squares + part * part
            inverse = lax.rsqrt(jnp.sum(squares, axis=1, keepdims=True) * (1.0 / width) + EPSILON)
            spread = lane_spread(inverse)
            spread_two = jnp.concatenate([spread, spread], axis=1)
            present = (slot == 0) | two
            r_buf[d, m, 0, slot] = jnp.where(present, spread, 0.0)
            for pair in range(pairs):
                cols = slice(pair * PAIR, (pair + 1) * PAIR)
                state = h_buf[d, m, 0, slot, :, cols].astype(F32)
                values = (state * spread_two * g_buf[d, 0, slot, 0:1, cols]).astype(BF16)
                v_buf[d, m, slot, :, cols] = values
                scaled_q = (q_buf[d, m, slot, :, cols].astype(F32) * g_buf[d, 0, slot, 1:2, cols]).astype(BF16)
                scaled_k = (k_buf[d, m, slot, :, cols].astype(F32) * g_buf[d, 0, slot, 2:3, cols]).astype(BF16)
                scores = dot(scaled_k, blocks_apart(scaled_q), 1, 1) * scale
                masked = jnp.where(allowed, scores, -1e30)
                top = jnp.max(masked, axis=0, keepdims=True)
                terms = jnp.where(allowed, jnp.exp(masked - top), 0.0)
                probs = terms * (1.0 / jnp.sum(terms, axis=0, keepdims=True))
                low = probs.astype(BF16)
                p_wide[d, m, slot, pair] = probs
                p_low[d, m, 0, slot, pair] = low
                mixed = dot(low, values, 0, 0)
                mixed = jnp.concatenate([mixed[:seq, :HEAD_DIM], mixed[seq:, HEAD_DIM:]], axis=1)
                h_buf[d, m, 0, slot + 1, :, cols] = (state + mixed).astype(BF16)

        @pl.when(t == 0)
        def _():
            pl.semaphore_wait(barrier, neighbours)

        @pl.when(core == 0)
        def _():
            for copy in operand_copies(d, m):
                copy.start()

    def chain(d, m):
        leading = jnp.where(d == 0, chip == chips - 1, chip == 0)

        @pl.when(leading)
        def _():
            seed(d, m).wait()
            length = lengths_ref[d, 0, m]
            sequence_at = lax.broadcasted_iota(jnp.int32, (seq, PAIR), 0)
            for pair in range(pairs):
                cols = slice(pair * PAIR, (pair + 1) * PAIR)
                drawn = e_buf[d, m, 0, :, cols].astype(F32)
                e_buf[d, m, 0, :, cols] = jnp.where(sequence_at < length, drawn, 0.0).astype(BF16)

        for copy in operand_copies(d, m):
            copy.wait_recv()

        @pl.when(jnp.logical_not(leading))
        def _():
            hop(d, m).wait_recv()

        @pl.loop(0, 4)
        def _(step):
            at = step - (2 - 2 * d)

            @pl.when((at >= 0) & (at <= 2))
            def _():
                stage_copy(d, m, at).start()

            whose = jnp.where(lax.div(step, 2) == d, 0, 1)
            slot = 1 - lax.rem(step, 2)
            total = jnp.zeros((seq, HEAD_DIM), F32)
            for pair in range(pairs):
                cols = slice(pair * PAIR, (pair + 1) * PAIR)
                grad = e_buf[d, m, step, :, cols]
                product = dot(p_low[d, m, whose, slot, pair], blocks_apart(grad), 1, 0)
                product = product * g_buf[d, whose, slot, 0:1, cols]
                x_buf[:, cols] = product
                weighed = product * h_buf[d, m, whose, slot, :, cols].astype(F32)
                total = total + (weighed[:, :HEAD_DIM] + weighed[:, HEAD_DIM:])
            inverse = r_buf[d, m, whose, slot]
            shift = lane_spread(jnp.sum(total, axis=1, keepdims=True) * (1.0 / width))
            shift = shift * inverse * inverse * inverse
            for tile in range(width // HEAD_DIM):
                cols = slice(tile * HEAD_DIM, (tile + 1) * HEAD_DIM)
                state = h_buf[d, m, whose, slot, :, cols].astype(F32)
                grad = e_buf[d, m, step, :, cols].astype(F32)
                e_buf[d, m, step + 1, :, cols] = (grad + (inverse * x_buf[:, cols] - state * shift)).astype(BF16)

        ending = jnp.where(d == 0, chip == 0, chip == chips - 1)

        @pl.when(jnp.logical_not(ending))
        def _():
            hop(d, m).start()

        @pl.when(d == 0)
        def _():
            stage_copy(d, m, 2).start()

    def gain_terms(d, m):
        two = second_layer(d)

        @pl.when(core == 0)
        def _():
            for at in range(3):
                stage_copy(d, m, at).wait_recv()

        out_copy(d, m).start()

        @pl.loop(0, 2)
        def _(slot):
            at = own_base(d) + 1 - slot
            inverse = r_buf[d, m, 0, slot]
            inverse_two = jnp.concatenate([inverse, inverse], axis=1)
            for pair in range(pairs):
                cols = slice(pair * PAIR, (pair + 1) * PAIR)
                grad = blocks_apart(e_buf[d, m, at, :, cols])
                value_grad = dot(p_low[d, m, 0, slot, pair], grad, 1, 0)
                normed = h_buf[d, m, 0, slot, :, cols].astype(F32) * inverse_two
                norm_term = jnp.sum(value_grad * normed, axis=0, keepdims=True)
                probs_grad = dot(v_buf[d, m, slot, :, cols], grad, 1, 1)
                probs = p_wide[d, m, slot, pair]
                delta = jnp.sum(probs * probs_grad, axis=0, keepdims=True)
                score_grad = (probs * (probs_grad - delta) * scale).astype(BF16)
                met = dot(score_grad, blocks_apart(q_buf[d, m, slot, :, cols]), 1, 0)
                shared = jnp.sum(met * k_buf[d, m, slot, :, cols].astype(F32), axis=0, keepdims=True)
                shared = jnp.where((slot == 0) | two, shared, 0.0)
                terms_ref[d, slot, 0:1, cols] += norm_term
                terms_ref[d, slot, 1:2, cols] += shared * g_buf[d, 0, slot, 2:3, cols]
                terms_ref[d, slot, 2:3, cols] += shared * g_buf[d, 0, slot, 1:2, cols]

    def scatter_copy(d, reducer, source):
        target = jnp.where(d == 0, place, sections - 1 - place)
        return pltpu.make_async_remote_copy(
            src_ref=sent_terms.at[d, :, reducer * chunk : (reducer + 1) * chunk],
            dst_ref=met_terms.at[d, source],
            send_sem=scatter_send.at[d, reducer],
            recv_sem=scatter_recv.at[d, source],
            device_id={"section": target, "dp": jnp.int32(reducer)},
            device_id_type=MESH,
        )

    def gather_copy(reducer, target):
        return pltpu.make_async_remote_copy(
            src_ref=final_terms.at[reducer],
            dst_ref=final_terms.at[reducer],
            send_sem=gather_send.at[target],
            recv_sem=gather_recv.at[reducer],
            device_id={"dp": jnp.int32(target)},
            device_id_type=MESH,
        )

    def scatter(d):
        for slot in range(2):
            for row in range(3):
                at = 3 * slot + row
                sent_terms[d, at : at + 1, :] = terms_ref[d, slot, row : row + 1, :]
        for reducer in range(reducers):

            @pl.when((d == 1) | (reducer != group))
            def _():
                scatter_copy(d, reducer, group).start()

    @pl.loop(0, 12)
    def _(t):
        later = lax.div(t - 4, 2)
        lead_unit = jnp.where(t < 4, lax.div(t, 2), jnp.where(t < 6, t - 2, jnp.where(t < 8, t - 6, later)))
        unit = jnp.where(leads, lead_unit, jnp.where(t < 4, t, later))
        odd = lax.rem(t, 2) == 1
        lead_chain = jnp.where(t < 4, odd, (t >= 8) & jnp.logical_not(odd))
        lead_terms = jnp.where(t < 8, t >= 6, odd)
        is_chain = jnp.where(leads, lead_chain, (t >= 4) & jnp.logical_not(odd))
        is_terms = jnp.where(leads, lead_terms, (t >= 4) & odd)
        d = jnp.where(unit < 2, first_direction, 1 - first_direction)
        m = lax.rem(unit, 2)

        @pl.when(jnp.logical_not(is_chain | is_terms))
        def _():
            prepare(d, m, t)

        @pl.when(is_chain & runner)
        def _():
            chain(d, m)

        @pl.when(is_terms)
        def _():
            gain_terms(d, m)

        @pl.when(is_terms & (m == 1))
        def _():
            scatter(d)

    @pl.when(group < reducers)
    def _():
        total = sent_terms[0, :, pl.ds(pl.multiple_of(group * chunk, chunk), chunk)]
        for other in range(groups):
            scatter_copy(1, 0, other).wait_recv()
            total = total + met_terms[1, other]
        for other in range(groups):

            @pl.when(other != group)
            def _():
                scatter_copy(0, 0, other).wait_recv()

        for other in range(groups):
            total = total + jnp.where(other == group, 0.0, met_terms[0, other])
        final_terms[group] = total * (1.0 / groups)
        for other in range(groups):

            @pl.when(other != group)
            def _():
                gather_copy(group, other).start()

    for reducer in range(reducers):

        @pl.when(reducer != group)
        def _():
            gather_copy(reducer, 0).wait_recv()

        for slot in range(2):
            for row in range(3):
                sums_ref[0, row, slot : slot + 1, reducer * chunk : (reducer + 1) * chunk] = final_terms[
                    reducer, 3 * slot + row : 3 * slot + row + 1, :
                ]

    for other in range(groups):

        @pl.when((group < reducers) & (other != group))
        def _():
            gather_copy(group, other).wait_send()

    for reducer in range(reducers):
        scatter_copy(1, reducer, group).wait_send()

        @pl.when(reducer != group)
        def _():
            scatter_copy(0, reducer, group).wait_send()

    for d in range(2):
        ending = (chip == 0) if d == 0 else (chip == chips - 1)
        for m in range(2):
            out_copy(d, m).wait()

            @pl.when(core == 0)
            def _():
                for copy in operand_copies(d, m):
                    copy.wait_send()

            @pl.when(runner)
            def _():
                for at in range(3):
                    stage_copy(d, m, at).wait_send()

            @pl.when(runner & jnp.logical_not(ending))
            def _():
                hop(d, m).wait_send()


def body(
    section_of_layer, lengths, layer_gains, saved_queries, saved_keys, block_inputs, cotangents
):
    sections = lax.axis_size("section")
    groups = lax.axis_size("dp")
    seq, width = block_inputs.shape[3:]
    pairs = width // PAIR
    anywhere = pl.BlockSpec(memory_space=pl.ANY)
    scalars = pl.BlockSpec(memory_space=pltpu.SMEM)
    vector = pl.BlockSpec(memory_space=pltpu.VMEM)
    dma = pltpu.SemaphoreType.DMA
    reducers = 5
    input_grads, sums = pl.pallas_call(
        functools.partial(kernel, sections),
        out_shape=(
            jax.ShapeDtypeStruct(block_inputs.shape, BF16),
            jax.ShapeDtypeStruct((1, 3, 2, width), F32),
        ),
        in_specs=[scalars, scalars, anywhere, anywhere, anywhere, anywhere, anywhere],
        out_specs=(anywhere, vector),
        scratch_shapes=[
            pltpu.VMEM((3, layer_gains.shape[0], width), F32),
            pltpu.VMEM((2, 2, 8, width), F32),
            pltpu.VMEM((2, 8, width), F32),
            pltpu.VMEM((2, groups, 8, width // reducers), F32),
            pltpu.VMEM((reducers, 8, width // reducers), F32),
            pltpu.VMEM((2, 2, 2, seq, width), BF16),
            pltpu.VMEM((2, 2, 2, seq, width), BF16),
            pltpu.VMEM((2, 2, 2, 3, seq, width), BF16),
            pltpu.VMEM((2, 2, 2, seq, width), BF16),
            pltpu.VMEM((2, 2, 2, pairs, seq, 2 * seq), F32),
            pltpu.VMEM((2, 2, 2, 2, pairs, seq, 2 * seq), BF16),
            pltpu.VMEM((2, 2, 2, 2, seq, HEAD_DIM), F32),
            pltpu.VMEM((2, 2, 5, seq, width), BF16),
            pltpu.VMEM((seq, width), F32),
            pltpu.VMEM((2, 2, 2, 8, width), F32),
            dma((2, 2, 5)),
            dma((2, 2)),
            dma((2, 2, 3)),
            dma((2, 2, 3)),
            dma((2, 2)),
            dma((2, 2)),
            dma((2, 2, 3)),
            dma((2, 2, 3)),
            dma((2, 2)),
            dma,
            dma((2, reducers)),
            dma((2, groups)),
            dma((groups,)),
            dma((reducers,)),
        ],
        compiler_params=pltpu.CompilerParams(
            collective_id=0, has_side_effects=True, vmem_limit_bytes=60000 * 1024
        ),
    )(
        section_of_layer,
        jnp.transpose(lengths, (0, 2, 1)),
        jnp.transpose(layer_gains, (1, 0, 2)),
        saved_queries,
        saved_keys,
        block_inputs,
        cotangents,
    )
    return (input_grads, jnp.transpose(sums, (0, 2, 1, 3)))


def solution(mesh):
    in_specs = (
        P(),
        P(None, None, "dp"),
        P(),
        P(None, "section", None, None, "dp", None),
        P(None, "section", None, None, "dp", None),
        P(None, "section", None, "dp", None),
        P(None, None, "dp", None),
    )
    out_specs = (P(None, "section", None, "dp", None), P("section", None, None, None))
    return jax.shard_map(body, mesh=mesh, in_specs=in_specs, out_specs=out_specs, check_vma=False)
```

```python
import functools
import math

import jax
import jax.numpy as jnp
from jax import lax
from jax.experimental import pallas as pl
from jax.experimental.pallas import tpu as pltpu
from jax.sharding import PartitionSpec as P

HEAD_DIM = 128
PAIR = 2 * HEAD_DIM
EPSILON = 1e-06
MESH = pl.DeviceIdType.MESH
F32 = jnp.float32
BF16 = jnp.bfloat16


def blocks_apart(pair):
    zero = jnp.zeros((pair.shape[0], HEAD_DIM), pair.dtype)
    upper = jnp.concatenate([pair[:, :HEAD_DIM], zero], axis=1)
    lower = jnp.concatenate([zero, pair[:, HEAD_DIM:]], axis=1)
    return jnp.concatenate([upper, lower], axis=0)


def dot(left, right, left_dim, right_dim):
    return lax.dot_general(
        left, right, (((left_dim,), (right_dim,)), ((), ())), preferred_element_type=F32
    )


def kernel(
    sections,
    layers_ref,
    lengths_ref,
    gains_hbm,
    queries_hbm,
    keys_hbm,
    inputs_hbm,
    cotangents_hbm,
    grads_hbm,
    sums_ref,
    gains_ref,
    terms_ref,
    sent_terms,
    met_terms,
    final_terms,
    q_buf,
    k_buf,
    h_buf,
    v_buf,
    p_wide,
    p_low,
    r_buf,
    e_buf,
    x_buf,
    g_buf,
    load_sems,
    seed_sems,
    op_send,
    op_recv,
    hop_send,
    hop_recv,
    set_send,
    set_recv,
    out_sems,
    gain_sem,
    scatter_send,
    scatter_recv,
    gather_send,
    gather_recv,
):
    place = lax.axis_index("section")
    group = lax.axis_index("dp")
    groups = scatter_recv.shape[1]
    reducers = gather_recv.shape[0]
    core = lax.rem(place, 2)
    chip = lax.div(place, 2)
    chips = sections // 2
    seq = q_buf.shape[3]
    width = q_buf.shape[4]
    pairs = width // PAIR
    layer_total = layers_ref.shape[0]
    chunk = width // reducers
    blocks = hop_recv.shape[2]
    block_rows = seq // blocks
    scale = 1.0 / math.sqrt(HEAD_DIM)
    partner = {"section": place + 1 - 2 * core}
    first_direction = jnp.where(chip >= chips // 2, 0, 1)
    leads = (chip == chips - 1) | (chip == 0)

    runner = core == 1
    barrier = pltpu.get_barrier_semaphore()
    pl.semaphore_signal(barrier, inc=1, device_id=partner, device_id_type=MESH)

    @pl.when(runner & (chip > 0))
    def _():
        pl.semaphore_signal(barrier, inc=1, device_id={"section": place - 2}, device_id_type=MESH)

    @pl.when(runner & (chip < chips - 1))
    def _():
        pl.semaphore_signal(barrier, inc=1, device_id={"section": place + 2}, device_id_type=MESH)

    for other in range(groups):

        @pl.when(other != group)
        def _():
            pl.semaphore_signal(barrier, inc=1, device_id={"dp": jnp.int32(other)}, device_id_type=MESH)

        pl.semaphore_signal(
            barrier,
            inc=1,
            device_id={"section": sections - 1 - place, "dp": jnp.int32(other)},
            device_id_type=MESH,
        )

    gain_load = pltpu.make_async_copy(gains_hbm, gains_ref, gain_sem)
    gain_load.start()

    def state_load(d, m):
        return pltpu.make_async_copy(inputs_hbm.at[d, 0, m], h_buf.at[d, m, 0, 0], load_sems.at[d, m, 0])

    def head_loads(d, m, slot):
        return (
            pltpu.make_async_copy(
                keys_hbm.at[d, 0, slot, m], k_buf.at[d, m, slot], load_sems.at[d, m, 1 + 2 * slot]
            ),
            pltpu.make_async_copy(
                queries_hbm.at[d, 0, slot, m], q_buf.at[d, m, slot], load_sems.at[d, m, 2 + 2 * slot]
            ),
        )

    def seed(d, m):
        return pltpu.make_async_copy(cotangents_hbm.at[d, m], e_buf.at[d, m, 0], seed_sems.at[d, m])

    for phase in range(2):
        d = first_direction if phase == 0 else 1 - first_direction
        for m in range(2):
            state_load(d, m).start()
            for slot in range(2):
                for copy in head_loads(d, m, slot):
                    copy.start()
            if phase == 0:

                @pl.when(leads & runner)
                def _():
                    seed(d, m).start()

    gain_load.wait()

    for d in range(2):
        for whose in range(2):
            at = place if whose == 0 else place + 1 - 2 * core
            block = at if d == 0 else sections - 1 - at
            before = jnp.int32(0)
            for layer in range(layer_total):
                before = before + jnp.where(layers_ref[layer] < block, 1, 0)
            for slot in range(2):
                layer = jnp.minimum(before + slot, layer_total - 1)
                for row in range(3):
                    g_buf[d, whose, slot, row : row + 1, :] = gains_ref[row, pl.ds(layer, 1), :]

    terms_ref[...] = jnp.zeros_like(terms_ref)
    sent_terms[...] = jnp.zeros_like(sent_terms)
    met_terms[0, group] = jnp.zeros((8, chunk), F32)

    def second_layer(d):
        block = jnp.where(d == 0, place, sections - 1 - place)
        count = jnp.int32(0)
        for layer in range(layer_total):
            count = count + jnp.where(layers_ref[layer] == block, 1, 0)
        return count == 2

    neighbours = 1 + core * (jnp.where(chip > 0, 1, 0) + jnp.where(chip < chips - 1, 1, 0))
    neighbours = neighbours + 2 * groups - 1

    def operand_copies(d, m):
        pieces = (
            (p_low.at[d, m, 0], p_low.at[d, m, 1]),
            (h_buf.at[d, m, 0, 0:2], h_buf.at[d, m, 1, 0:2]),
            (r_buf.at[d, m, 0], r_buf.at[d, m, 1]),
        )
        return [
            pltpu.make_async_remote_copy(
                src_ref=source,
                dst_ref=target,
                send_sem=op_send.at[d, m, at],
                recv_sem=op_recv.at[d, m, at],
                device_id=partner,
                device_id_type=MESH,
            )
            for at, (source, target) in enumerate(pieces)
        ]

    def hop(d, m, block):
        step = jnp.where(d == 0, -2, 2)
        low = seq - (block + 1) * block_rows
        return pltpu.make_async_remote_copy(
            src_ref=e_buf.at[d, m, 4, low : low + block_rows],
            dst_ref=e_buf.at[d, m, 0, low : low + block_rows],
            send_sem=hop_send.at[d, m, block],
            recv_sem=hop_recv.at[d, m, block],
            device_id={"section": place + step},
            device_id_type=MESH,
        )

    def stage_copy(d, m, at):
        return pltpu.make_async_remote_copy(
            src_ref=e_buf.at[d, m, 2 - 2 * d + at],
            dst_ref=e_buf.at[d, m, at],
            send_sem=set_send.at[d, m, at],
            recv_sem=set_recv.at[d, m, at],
            device_id=partner,
            device_id_type=MESH,
        )

    def own_base(d):
        return core * 2 * d

    def out_copy(d, m):
        return pltpu.make_async_copy(e_buf.at[d, m, own_base(d) + 2], grads_hbm.at[d, 0, m], out_sems.at[d, m])

    def lane_spread(column):
        return jnp.broadcast_to(column, (seq, HEAD_DIM))

    def prepare(d, m, t):
        two = second_layer(d)
        state_load(d, m).wait()
        length = lengths_ref[d, 0, m]
        key_at = lax.broadcasted_iota(jnp.int32, (seq, 2 * seq), 0)
        query_at = lax.rem(lax.broadcasted_iota(jnp.int32, (seq, 2 * seq), 1), seq)
        allowed = (key_at <= query_at) & (key_at < length)

        @pl.loop(0, 2)
        def _(slot):
            for copy in head_loads(d, m, slot):
                copy.wait()
            squares = jnp.zeros((seq, HEAD_DIM), F32)
            for tile in range(width // HEAD_DIM):
                part = h_buf[d, m, 0, slot, :, tile * HEAD_DIM : (tile + 1) * HEAD_DIM].astype(F32)
                squares = squares + part * part
            inverse = lax.rsqrt(jnp.sum(squares, axis=1, keepdims=True) * (1.0 / width) + EPSILON)
            spread = lane_spread(inverse)
            spread_two = jnp.concatenate([spread, spread], axis=1)
            present = (slot == 0) | two
            r_buf[d, m, 0, slot] = jnp.where(present, spread, 0.0)
            for pair in range(pairs):
                cols = slice(pair * PAIR, (pair + 1) * PAIR)
                state = h_buf[d, m, 0, slot, :, cols].astype(F32)
                values = (state * spread_two * g_buf[d, 0, slot, 0:1, cols]).astype(BF16)
                v_buf[d, m, slot, :, cols] = values
                scaled_q = (q_buf[d, m, slot, :, cols].astype(F32) * g_buf[d, 0, slot, 1:2, cols]).astype(BF16)
                scaled_k = (k_buf[d, m, slot, :, cols].astype(F32) * g_buf[d, 0, slot, 2:3, cols]).astype(BF16)
                scores = dot(scaled_k, blocks_apart(scaled_q), 1, 1) * scale
                masked = jnp.where(allowed, scores, -1e30)
                top = jnp.max(masked, axis=0, keepdims=True)
                terms = jnp.where(allowed, jnp.exp(masked - top), 0.0)
                probs = terms * (1.0 / jnp.sum(terms, axis=0, keepdims=True))
                low = probs.astype(BF16)
                p_wide[d, m, slot, pair] = probs
                p_low[d, m, 0, slot, pair] = low
                mixed = dot(low, values, 0, 0)
                mixed = jnp.concatenate([mixed[:seq, :HEAD_DIM], mixed[seq:, HEAD_DIM:]], axis=1)
                h_buf[d, m, 0, slot + 1, :, cols] = (state + mixed).astype(BF16)

        @pl.when(t == 0)
        def _():
            pl.semaphore_wait(barrier, neighbours)

        @pl.when(core == 0)
        def _():
            for copy in operand_copies(d, m):
                copy.start()

    def chain_block(d, m, block, leading, ending):
        low = seq - (block + 1) * block_rows
        high = low + block_rows

        @pl.when(jnp.logical_not(leading))
        def _():
            hop(d, m, block).wait_recv()

        @pl.loop(0, 4)
        def _(step):
            if block == blocks - 1:
                at = step - (2 - 2 * d)

                @pl.when((at >= 0) & (at <= 2))
                def _():
                    stage_copy(d, m, at).start()

            whose = jnp.where(lax.div(step, 2) == d, 0, 1)
            slot = 1 - lax.rem(step, 2)
            total = jnp.zeros((block_rows, HEAD_DIM), F32)
            for pair in range(pairs):
                cols = slice(pair * PAIR, (pair + 1) * PAIR)
                grad = e_buf[d, m, step, low:seq, cols]
                if low > 0:
                    grad = jnp.concatenate([jnp.zeros((low, PAIR), BF16), grad], axis=0)
                product = dot(p_low[d, m, whose, slot, pair, low:high, :], blocks_apart(grad), 1, 0)
                product = product * g_buf[d, whose, slot, 0:1, cols]
                x_buf[low:high, cols] = product
                weighed = product * h_buf[d, m, whose, slot, low:high, cols].astype(F32)
                total = total + (weighed[:, :HEAD_DIM] + weighed[:, HEAD_DIM:])
            inverse = r_buf[d, m, whose, slot, low:high]
            shift = jnp.sum(total, axis=1, keepdims=True) * (1.0 / width)
            shift = jnp.broadcast_to(shift, (block_rows, HEAD_DIM)) * inverse * inverse * inverse
            for tile in range(width // HEAD_DIM):
                cols = slice(tile * HEAD_DIM, (tile + 1) * HEAD_DIM)
                state = h_buf[d, m, whose, slot, low:high, cols].astype(F32)
                grad = e_buf[d, m, step, low:high, cols].astype(F32)
                grad = grad + (inverse * x_buf[low:high, cols] - state * shift)
                e_buf[d, m, step + 1, low:high, cols] = grad.astype(BF16)

        @pl.when(jnp.logical_not(ending))
        def _():
            hop(d, m, block).start()

    def chain(d, m):
        leading = jnp.where(d == 0, chip == chips - 1, chip == 0)

        @pl.when(leading)
        def _():
            seed(d, m).wait()
            length = lengths_ref[d, 0, m]
            sequence_at = lax.broadcasted_iota(jnp.int32, (seq, PAIR), 0)
            for pair in range(pairs):
                cols = slice(pair * PAIR, (pair + 1) * PAIR)
                drawn = e_buf[d, m, 0, :, cols].astype(F32)
                e_buf[d, m, 0, :, cols] = jnp.where(sequence_at < length, drawn, 0.0).astype(BF16)

        for copy in operand_copies(d, m):
            copy.wait_recv()

        ending = jnp.where(d == 0, chip == 0, chip == chips - 1)
        for block in range(blocks):
            chain_block(d, m, block, leading, ending)

        @pl.when(d == 0)
        def _():
            stage_copy(d, m, 2).start()

    def gain_terms(d, m):
        two = second_layer(d)

        @pl.when(core == 0)
        def _():
            for at in range(3):
                stage_copy(d, m, at).wait_recv()

        out_copy(d, m).start()

        @pl.loop(0, 2)
        def _(slot):
            at = own_base(d) + 1 - slot
            inverse = r_buf[d, m, 0, slot]
            inverse_two = jnp.concatenate([inverse, inverse], axis=1)
            for pair in range(pairs):
                cols = slice(pair * PAIR, (pair + 1) * PAIR)
                grad = blocks_apart(e_buf[d, m, at, :, cols])
                value_grad = dot(p_low[d, m, 0, slot, pair], grad, 1, 0)
                normed = h_buf[d, m, 0, slot, :, cols].astype(F32) * inverse_two
                norm_term = jnp.sum(value_grad * normed, axis=0, keepdims=True)
                probs_grad = dot(v_buf[d, m, slot, :, cols], grad, 1, 1)
                probs = p_wide[d, m, slot, pair]
                delta = jnp.sum(probs * probs_grad, axis=0, keepdims=True)
                score_grad = (probs * (probs_grad - delta) * scale).astype(BF16)
                met = dot(score_grad, blocks_apart(q_buf[d, m, slot, :, cols]), 1, 0)
                shared = jnp.sum(met * k_buf[d, m, slot, :, cols].astype(F32), axis=0, keepdims=True)
                shared = jnp.where((slot == 0) | two, shared, 0.0)
                terms_ref[d, slot, 0:1, cols] += norm_term
                terms_ref[d, slot, 1:2, cols] += shared * g_buf[d, 0, slot, 2:3, cols]
                terms_ref[d, slot, 2:3, cols] += shared * g_buf[d, 0, slot, 1:2, cols]

    def scatter_copy(d, reducer, source):
        target = jnp.where(d == 0, place, sections - 1 - place)
        return pltpu.make_async_remote_copy(
            src_ref=sent_terms.at[d, :, reducer * chunk : (reducer + 1) * chunk],
            dst_ref=met_terms.at[d, source],
            send_sem=scatter_send.at[d, reducer],
            recv_sem=scatter_recv.at[d, source],
            device_id={"section": target, "dp": jnp.int32(reducer)},
            device_id_type=MESH,
        )

    def gather_copy(reducer, target):
        return pltpu.make_async_remote_copy(
            src_ref=final_terms.at[reducer],
            dst_ref=final_terms.at[reducer],
            send_sem=gather_send.at[target],
            recv_sem=gather_recv.at[reducer],
            device_id={"dp": jnp.int32(target)},
            device_id_type=MESH,
        )

    def scatter(d):
        for slot in range(2):
            for row in range(3):
                at = 3 * slot + row
                sent_terms[d, at : at + 1, :] = terms_ref[d, slot, row : row + 1, :]
        for reducer in range(reducers):

            @pl.when((d == 1) | (reducer != group))
            def _():
                scatter_copy(d, reducer, group).start()

    @pl.loop(0, 12)
    def _(t):
        later = lax.div(t - 4, 2)
        lead_unit = jnp.where(t < 4, lax.div(t, 2), jnp.where(t < 6, t - 2, jnp.where(t < 8, t - 6, later)))
        unit = jnp.where(leads, lead_unit, jnp.where(t < 4, t, later))
        odd = lax.rem(t, 2) == 1
        lead_chain = jnp.where(t < 4, odd, (t >= 8) & jnp.logical_not(odd))
        lead_terms = jnp.where(t < 8, t >= 6, odd)
        is_chain = jnp.where(leads, lead_chain, (t >= 4) & jnp.logical_not(odd))
        is_terms = jnp.where(leads, lead_terms, (t >= 4) & odd)
        d = jnp.where(unit < 2, first_direction, 1 - first_direction)
        m = lax.rem(unit, 2)

        @pl.when(jnp.logical_not(is_chain | is_terms))
        def _():
            prepare(d, m, t)

        @pl.when(is_chain & runner)
        def _():
            chain(d, m)

        @pl.when(is_terms)
        def _():
            gain_terms(d, m)

        @pl.when(is_terms & (m == 1))
        def _():
            scatter(d)

    @pl.when(group < reducers)
    def _():
        total = sent_terms[0, :, pl.ds(pl.multiple_of(group * chunk, chunk), chunk)]
        for other in range(groups):
            scatter_copy(1, 0, other).wait_recv()
            total = total + met_terms[1, other]
        for other in range(groups):

            @pl.when(other != group)
            def _():
                scatter_copy(0, 0, other).wait_recv()

        for other in range(groups):
            total = total + jnp.where(other == group, 0.0, met_terms[0, other])
        final_terms[group] = total * (1.0 / groups)
        for other in range(groups):

            @pl.when(other != group)
            def _():
                gather_copy(group, other).start()

    for reducer in range(reducers):

        @pl.when(reducer != group)
        def _():
            gather_copy(reducer, 0).wait_recv()

        for slot in range(2):
            for row in range(3):
                sums_ref[0, row, slot : slot + 1, reducer * chunk : (reducer + 1) * chunk] = final_terms[
                    reducer, 3 * slot + row : 3 * slot + row + 1, :
                ]

    for other in range(groups):

        @pl.when((group < reducers) & (other != group))
        def _():
            gather_copy(group, other).wait_send()

    for reducer in range(reducers):
        scatter_copy(1, reducer, group).wait_send()

        @pl.when(reducer != group)
        def _():
            scatter_copy(0, reducer, group).wait_send()

    for d in range(2):
        ending = (chip == 0) if d == 0 else (chip == chips - 1)
        for m in range(2):
            out_copy(d, m).wait()

            @pl.when(core == 0)
            def _():
                for copy in operand_copies(d, m):
                    copy.wait_send()

            @pl.when(runner)
            def _():
                for at in range(3):
                    stage_copy(d, m, at).wait_send()

            @pl.when(runner & jnp.logical_not(ending))
            def _():
                for block in range(blocks):
                    hop(d, m, block).wait_send()


def body(
    section_of_layer, lengths, layer_gains, saved_queries, saved_keys, block_inputs, cotangents
):
    sections = lax.axis_size("section")
    groups = lax.axis_size("dp")
    seq, width = block_inputs.shape[3:]
    pairs = width // PAIR
    anywhere = pl.BlockSpec(memory_space=pl.ANY)
    scalars = pl.BlockSpec(memory_space=pltpu.SMEM)
    vector = pl.BlockSpec(memory_space=pltpu.VMEM)
    dma = pltpu.SemaphoreType.DMA
    reducers = 5
    row_blocks = 2
    input_grads, sums = pl.pallas_call(
        functools.partial(kernel, sections),
        out_shape=(
            jax.ShapeDtypeStruct(block_inputs.shape, BF16),
            jax.ShapeDtypeStruct((1, 3, 2, width), F32),
        ),
        in_specs=[scalars, scalars, anywhere, anywhere, anywhere, anywhere, anywhere],
        out_specs=(anywhere, vector),
        scratch_shapes=[
            pltpu.VMEM((3, layer_gains.shape[0], width), F32),
            pltpu.VMEM((2, 2, 8, width), F32),
            pltpu.VMEM((2, 8, width), F32),
            pltpu.VMEM((2, groups, 8, width // reducers), F32),
            pltpu.VMEM((reducers, 8, width // reducers), F32),
            pltpu.VMEM((2, 2, 2, seq, width), BF16),
            pltpu.VMEM((2, 2, 2, seq, width), BF16),
            pltpu.VMEM((2, 2, 2, 3, seq, width), BF16),
            pltpu.VMEM((2, 2, 2, seq, width), BF16),
            pltpu.VMEM((2, 2, 2, pairs, seq, 2 * seq), F32),
            pltpu.VMEM((2, 2, 2, 2, pairs, seq, 2 * seq), BF16),
            pltpu.VMEM((2, 2, 2, 2, seq, HEAD_DIM), F32),
            pltpu.VMEM((2, 2, 5, seq, width), BF16),
            pltpu.VMEM((seq, width), F32),
            pltpu.VMEM((2, 2, 2, 8, width), F32),
            dma((2, 2, 5)),
            dma((2, 2)),
            dma((2, 2, 3)),
            dma((2, 2, 3)),
            dma((2, 2, row_blocks)),
            dma((2, 2, row_blocks)),
            dma((2, 2, 3)),
            dma((2, 2, 3)),
            dma((2, 2)),
            dma,
            dma((2, reducers)),
            dma((2, groups)),
            dma((groups,)),
            dma((reducers,)),
        ],
        compiler_params=pltpu.CompilerParams(
            collective_id=0, has_side_effects=True, vmem_limit_bytes=60000 * 1024
        ),
    )(
        section_of_layer,
        jnp.transpose(lengths, (0, 2, 1)),
        jnp.transpose(layer_gains, (1, 0, 2)),
        saved_queries,
        saved_keys,
        block_inputs,
        cotangents,
    )
    return (input_grads, jnp.transpose(sums, (0, 2, 1, 3)))


def solution(mesh):
    in_specs = (
        P(),
        P(None, None, "dp"),
        P(),
        P(None, "section", None, None, "dp", None),
        P(None, "section", None, None, "dp", None),
        P(None, "section", None, "dp", None),
        P(None, None, "dp", None),
    )
    out_specs = (P(None, "section", None, "dp", None), P("section", None, None, None))
    return jax.shard_map(body, mesh=mesh, in_specs=in_specs, out_specs=out_specs, check_vma=False)
```

```python
import functools
import math

import jax
import jax.numpy as jnp
from jax import lax
from jax.experimental import pallas as pl
from jax.experimental.pallas import tpu as pltpu
from jax.sharding import PartitionSpec as P

HEAD_DIM = 128
PAIR = 2 * HEAD_DIM
EPSILON = 1e-06
MESH = pl.DeviceIdType.MESH
F32 = jnp.float32
BF16 = jnp.bfloat16


def blocks_apart(pair):
    zero = jnp.zeros((pair.shape[0], HEAD_DIM), pair.dtype)
    upper = jnp.concatenate([pair[:, :HEAD_DIM], zero], axis=1)
    lower = jnp.concatenate([zero, pair[:, HEAD_DIM:]], axis=1)
    return jnp.concatenate([upper, lower], axis=0)


def dot(left, right, left_dim, right_dim):
    return lax.dot_general(
        left, right, (((left_dim,), (right_dim,)), ((), ())), preferred_element_type=F32
    )


def kernel(
    sections,
    layers_ref,
    lengths_ref,
    gains_hbm,
    queries_hbm,
    keys_hbm,
    inputs_hbm,
    cotangents_hbm,
    grads_hbm,
    sums_ref,
    gains_ref,
    terms_ref,
    sent_terms,
    met_terms,
    final_terms,
    q_buf,
    k_buf,
    h_low,
    h_high,
    v_buf,
    p_wide,
    p_low,
    r_buf,
    e_even,
    e_odd,
    x_buf,
    g_buf,
    load_sems,
    seed_sems,
    op_send,
    op_recv,
    hop_send,
    hop_recv,
    set_send,
    set_recv,
    out_sems,
    gain_sem,
    scatter_send,
    scatter_recv,
    gather_send,
    gather_recv,
):
    place = lax.axis_index("section")
    group = lax.axis_index("dp")
    groups = scatter_recv.shape[1]
    reducers = gather_recv.shape[0]
    core = lax.rem(place, 2)
    chip = lax.div(place, 2)
    chips = sections // 2
    seq = q_buf.shape[3]
    width = q_buf.shape[4]
    pairs = width // PAIR
    layer_total = layers_ref.shape[0]
    chunk = width // reducers
    blocks = hop_recv.shape[2]
    block_rows = seq // blocks
    scale = 1.0 / math.sqrt(HEAD_DIM)
    partner = {"section": place + 1 - 2 * core}
    first_direction = jnp.where(chip >= chips // 2, 0, 1)
    leads = (chip == chips - 1) | (chip == 0)

    runner = core == 1
    barrier = pltpu.get_barrier_semaphore()
    pl.semaphore_signal(barrier, inc=1, device_id=partner, device_id_type=MESH)

    @pl.when(runner & (chip > 0))
    def _():
        pl.semaphore_signal(barrier, inc=1, device_id={"section": place - 2}, device_id_type=MESH)

    @pl.when(runner & (chip < chips - 1))
    def _():
        pl.semaphore_signal(barrier, inc=1, device_id={"section": place + 2}, device_id_type=MESH)

    for other in range(groups):

        @pl.when(other != group)
        def _():
            pl.semaphore_signal(barrier, inc=1, device_id={"dp": jnp.int32(other)}, device_id_type=MESH)

        pl.semaphore_signal(
            barrier,
            inc=1,
            device_id={"section": sections - 1 - place, "dp": jnp.int32(other)},
            device_id_type=MESH,
        )

    gain_load = pltpu.make_async_copy(gains_hbm, gains_ref, gain_sem)
    gain_load.start()

    def state_load(d, m):
        return pltpu.make_async_copy(inputs_hbm.at[d, 0, m], h_low.at[d, m, 0], load_sems.at[d, m, 0])

    def head_loads(d, m, slot):
        return (
            pltpu.make_async_copy(
                keys_hbm.at[d, 0, slot, m], k_buf.at[d, m, slot], load_sems.at[d, m, 1 + 2 * slot]
            ),
            pltpu.make_async_copy(
                queries_hbm.at[d, 0, slot, m], q_buf.at[d, m, slot], load_sems.at[d, m, 2 + 2 * slot]
            ),
        )

    def seed(d, m):
        return pltpu.make_async_copy(cotangents_hbm.at[d, m], e_even.at[d, m, 0], seed_sems.at[d, m])

    for phase in range(2):
        d = first_direction if phase == 0 else 1 - first_direction
        for m in range(2):
            state_load(d, m).start()
            for slot in range(2):
                for copy in head_loads(d, m, slot):
                    copy.start()
            if phase == 0:

                @pl.when(leads & runner)
                def _():
                    seed(d, m).start()

    gain_load.wait()

    for d in range(2):
        for whose in range(2):
            at = place if whose == 0 else place + 1 - 2 * core
            block = at if d == 0 else sections - 1 - at
            before = jnp.int32(0)
            for layer in range(layer_total):
                before = before + jnp.where(layers_ref[layer] < block, 1, 0)
            for slot in range(2):
                layer = jnp.minimum(before + slot, layer_total - 1)
                for row in range(3):
                    g_buf[d, whose, slot, row : row + 1, :] = gains_ref[row, pl.ds(layer, 1), :]

    terms_ref[...] = jnp.zeros_like(terms_ref)
    sent_terms[...] = jnp.zeros_like(sent_terms)
    met_terms[0, group] = jnp.zeros((8, chunk), F32)

    def second_layer(d):
        block = jnp.where(d == 0, place, sections - 1 - place)
        count = jnp.int32(0)
        for layer in range(layer_total):
            count = count + jnp.where(layers_ref[layer] == block, 1, 0)
        return count == 2

    neighbours = 1 + core * (jnp.where(chip > 0, 1, 0) + jnp.where(chip < chips - 1, 1, 0))
    neighbours = neighbours + 2 * groups - 1

    def operand_copies(d, m):
        pieces = (
            (p_low.at[d, m, 0], p_low.at[d, m, 1]),
            (h_low.at[d, m, 0], h_low.at[d, m, 1]),
            (h_high.at[d, m, 0], h_high.at[d, m, 1]),
            (r_buf.at[d, m, 0], r_buf.at[d, m, 1]),
        )
        return [
            pltpu.make_async_remote_copy(
                src_ref=source,
                dst_ref=target,
                send_sem=op_send.at[d, m, at],
                recv_sem=op_recv.at[d, m, at],
                device_id=partner,
                device_id_type=MESH,
            )
            for at, (source, target) in enumerate(pieces)
        ]

    def hop(d, m, block):
        step = jnp.where(d == 0, -2, 2)
        low = seq - (block + 1) * block_rows
        return pltpu.make_async_remote_copy(
            src_ref=e_even.at[d, m, 2, low : low + block_rows],
            dst_ref=e_even.at[d, m, 0, low : low + block_rows],
            send_sem=hop_send.at[d, m, block],
            recv_sem=hop_recv.at[d, m, block],
            device_id={"section": place + step},
            device_id_type=MESH,
        )

    def stage_copy(d, m, at):
        held = (e_even.at[d, m, 1 - d], e_odd.at[d, m, 1 - d], e_even.at[d, m, 2 - d])[at]
        met = (e_even.at[d, m, 0], e_odd.at[d, m, 0], e_even.at[d, m, 1])[at]
        return pltpu.make_async_remote_copy(
            src_ref=held,
            dst_ref=met,
            send_sem=set_send.at[d, m, at],
            recv_sem=set_recv.at[d, m, at],
            device_id=partner,
            device_id_type=MESH,
        )

    def own_base(d):
        return core * d

    def out_copy(d, m):
        return pltpu.make_async_copy(e_even.at[d, m, own_base(d) + 1], grads_hbm.at[d, 0, m], out_sems.at[d, m])

    def lane_spread(column):
        return jnp.broadcast_to(column, (seq, HEAD_DIM))

    def prepare(d, m, t):
        two = second_layer(d)
        state_load(d, m).wait()
        length = lengths_ref[d, 0, m]
        key_at = lax.broadcasted_iota(jnp.int32, (seq, 2 * seq), 0)
        query_at = lax.rem(lax.broadcasted_iota(jnp.int32, (seq, 2 * seq), 1), seq)
        allowed = (key_at <= query_at) & (key_at < length)

        for slot in range(2):
            held = (h_low, h_high)[slot]
            for copy in head_loads(d, m, slot):
                copy.wait()
            squares = jnp.zeros((seq, HEAD_DIM), F32)
            for tile in range(width // HEAD_DIM):
                part = held[d, m, 0, :, tile * HEAD_DIM : (tile + 1) * HEAD_DIM].astype(F32)
                squares = squares + part * part
            inverse = lax.rsqrt(jnp.sum(squares, axis=1, keepdims=True) * (1.0 / width) + EPSILON)
            spread = lane_spread(inverse)
            spread_two = jnp.concatenate([spread, spread], axis=1)
            r_buf[d, m, 0, slot] = spread if slot == 0 else jnp.where(two, spread, 0.0)
            for pair in range(pairs):
                cols = slice(pair * PAIR, (pair + 1) * PAIR)
                state = held[d, m, 0, :, cols].astype(F32)
                values = (state * spread_two * g_buf[d, 0, slot, 0:1, cols]).astype(BF16)
                v_buf[d, m, slot, :, cols] = values
                scaled_q = (q_buf[d, m, slot, :, cols].astype(F32) * g_buf[d, 0, slot, 1:2, cols]).astype(BF16)
                scaled_k = (k_buf[d, m, slot, :, cols].astype(F32) * g_buf[d, 0, slot, 2:3, cols]).astype(BF16)
                scores = dot(scaled_k, blocks_apart(scaled_q), 1, 1) * scale
                masked = jnp.where(allowed, scores, -1e30)
                top = jnp.max(masked, axis=0, keepdims=True)
                terms = jnp.where(allowed, jnp.exp(masked - top), 0.0)
                probs = terms * (1.0 / jnp.sum(terms, axis=0, keepdims=True))
                low = probs.astype(BF16)
                p_wide[d, m, slot, pair] = probs
                p_low[d, m, 0, slot, pair] = low
                if slot == 0:
                    mixed = dot(low, values, 0, 0)
                    mixed = jnp.concatenate([mixed[:seq, :HEAD_DIM], mixed[seq:, HEAD_DIM:]], axis=1)
                    h_high[d, m, 0, :, cols] = (state + mixed).astype(BF16)

        @pl.when(t == 0)
        def _():
            pl.semaphore_wait(barrier, neighbours)

        @pl.when(core == 0)
        def _():
            for copy in operand_copies(d, m):
                copy.start()

    def chain_block(d, m, block, leading, ending):
        low = seq - (block + 1) * block_rows
        high = low + block_rows

        @pl.when(jnp.logical_not(leading))
        def _():
            hop(d, m, block).wait_recv()

        @pl.loop(0, 2)
        def _(visit):
            whose = jnp.where(visit == d, 0, 1)
            if block == 0:

                @pl.when(visit == 1 - d)
                def _():
                    for copy in operand_copies(d, m):
                        copy.wait_recv()

            for slot in (1, 0):
                if block == blocks - 1:
                    if slot == 1:

                        @pl.when(visit == 1 - d)
                        def _():
                            stage_copy(d, m, 0).start()

                        @pl.when(visit > 1 - d)
                        def _():
                            stage_copy(d, m, 2).start()

                    else:

                        @pl.when(visit == 1 - d)
                        def _():
                            stage_copy(d, m, 1).start()

                before, after = (e_odd, e_even) if slot == 0 else (e_even, e_odd)
                held = (h_low, h_high)[slot]
                onward = visit + 1 - slot
                total = jnp.zeros((block_rows, HEAD_DIM), F32)
                for pair in range(pairs):
                    cols = slice(pair * PAIR, (pair + 1) * PAIR)
                    grad = before[d, m, visit, low:seq, cols]
                    if low > 0:
                        grad = jnp.concatenate([jnp.zeros((low, PAIR), BF16), grad], axis=0)
                    product = dot(p_low[d, m, whose, slot, pair, low:high, :], blocks_apart(grad), 1, 0)
                    product = product * g_buf[d, whose, slot, 0:1, cols]
                    x_buf[low:high, cols] = product
                    weighed = product * held[d, m, whose, low:high, cols].astype(F32)
                    total = total + (weighed[:, :HEAD_DIM] + weighed[:, HEAD_DIM:])
                inverse = r_buf[d, m, whose, slot, low:high]
                shift = jnp.sum(total, axis=1, keepdims=True) * (1.0 / width)
                shift = jnp.broadcast_to(shift, (block_rows, HEAD_DIM)) * inverse * inverse * inverse
                for tile in range(width // HEAD_DIM):
                    cols = slice(tile * HEAD_DIM, (tile + 1) * HEAD_DIM)
                    state = held[d, m, whose, low:high, cols].astype(F32)
                    grad = before[d, m, visit, low:high, cols].astype(F32)
                    grad = grad + (inverse * x_buf[low:high, cols] - state * shift)
                    after[d, m, onward, low:high, cols] = grad.astype(BF16)

        @pl.when(jnp.logical_not(ending))
        def _():
            hop(d, m, block).start()

    def chain(d, m):
        leading = jnp.where(d == 0, chip == chips - 1, chip == 0)

        @pl.when(leading)
        def _():
            seed(d, m).wait()
            length = lengths_ref[d, 0, m]
            sequence_at = lax.broadcasted_iota(jnp.int32, (seq, PAIR), 0)
            for pair in range(pairs):
                cols = slice(pair * PAIR, (pair + 1) * PAIR)
                drawn = e_even[d, m, 0, :, cols].astype(F32)
                e_even[d, m, 0, :, cols] = jnp.where(sequence_at < length, drawn, 0.0).astype(BF16)

        ending = jnp.where(d == 0, chip == 0, chip == chips - 1)
        for block in range(blocks):
            chain_block(d, m, block, leading, ending)

        @pl.when(d == 0)
        def _():
            stage_copy(d, m, 2).start()

    def gain_terms(d, m):
        two = second_layer(d)

        @pl.when(core == 0)
        def _():
            for at in range(3):
                stage_copy(d, m, at).wait_recv()

        out_copy(d, m).start()

        for slot in range(2):
            held = (h_low, h_high)[slot]
            stage = (e_odd, e_even)[slot]
            inverse = r_buf[d, m, 0, slot]
            inverse_two = jnp.concatenate([inverse, inverse], axis=1)
            for pair in range(pairs):
                cols = slice(pair * PAIR, (pair + 1) * PAIR)
                grad = blocks_apart(stage[d, m, own_base(d), :, cols])
                value_grad = dot(p_low[d, m, 0, slot, pair], grad, 1, 0)
                normed = held[d, m, 0, :, cols].astype(F32) * inverse_two
                norm_term = jnp.sum(value_grad * normed, axis=0, keepdims=True)
                probs_grad = dot(v_buf[d, m, slot, :, cols], grad, 1, 1)
                probs = p_wide[d, m, slot, pair]
                delta = jnp.sum(probs * probs_grad, axis=0, keepdims=True)
                score_grad = (probs * (probs_grad - delta) * scale).astype(BF16)
                met = dot(score_grad, blocks_apart(q_buf[d, m, slot, :, cols]), 1, 0)
                shared = jnp.sum(met * k_buf[d, m, slot, :, cols].astype(F32), axis=0, keepdims=True)
                shared = shared if slot == 0 else jnp.where(two, shared, 0.0)
                terms_ref[d, slot, 0:1, cols] += norm_term
                terms_ref[d, slot, 1:2, cols] += shared * g_buf[d, 0, slot, 2:3, cols]
                terms_ref[d, slot, 2:3, cols] += shared * g_buf[d, 0, slot, 1:2, cols]

    def scatter_copy(d, reducer, source):
        target = jnp.where(d == 0, place, sections - 1 - place)
        return pltpu.make_async_remote_copy(
            src_ref=sent_terms.at[d, :, reducer * chunk : (reducer + 1) * chunk],
            dst_ref=met_terms.at[d, source],
            send_sem=scatter_send.at[d, reducer],
            recv_sem=scatter_recv.at[d, source],
            device_id={"section": target, "dp": jnp.int32(reducer)},
            device_id_type=MESH,
        )

    def gather_copy(reducer, target):
        return pltpu.make_async_remote_copy(
            src_ref=final_terms.at[reducer],
            dst_ref=final_terms.at[reducer],
            send_sem=gather_send.at[target],
            recv_sem=gather_recv.at[reducer],
            device_id={"dp": jnp.int32(target)},
            device_id_type=MESH,
        )

    def scatter(d):
        for slot in range(2):
            for row in range(3):
                at = 3 * slot + row
                sent_terms[d, at : at + 1, :] = terms_ref[d, slot, row : row + 1, :]
        for reducer in range(reducers):

            @pl.when((d == 1) | (reducer != group))
            def _():
                scatter_copy(d, reducer, group).start()

    middle = (chip == chips // 2) | (chip == chips // 2 - 1)

    @pl.loop(0, 12)
    def _(t):
        odd = lax.rem(t, 2) == 1
        lead_unit = jnp.where(t < 4, lax.div(t, 2), jnp.where(t < 6, t - 2, jnp.where(t < 8, t - 6, lax.div(t - 4, 2))))
        other_unit = 2 * lax.div(t - 4, 4) + lax.rem(t - 4, 2)
        late_unit = jnp.where(middle, lax.rem(t, 4), other_unit)
        unit = jnp.where(leads, lead_unit, jnp.where(t < 4, t, late_unit))
        lead_chain = jnp.where(t < 4, odd, (t >= 8) & jnp.logical_not(odd))
        lead_terms = jnp.where(t < 8, t >= 6, odd)
        late_terms = jnp.where(middle, t >= 8, lax.rem(t, 4) >= 2)
        is_chain = jnp.where(leads, lead_chain, (t >= 4) & jnp.logical_not(late_terms))
        is_terms = jnp.where(leads, lead_terms, (t >= 4) & late_terms)
        d = jnp.where(unit < 2, first_direction, 1 - first_direction)
        m = lax.rem(unit, 2)

        @pl.when(jnp.logical_not(is_chain | is_terms))
        def _():
            prepare(d, m, t)

        @pl.when(is_chain & runner)
        def _():
            chain(d, m)

        @pl.when(is_terms)
        def _():
            gain_terms(d, m)

        @pl.when(is_terms & (m == 1))
        def _():
            scatter(d)

    @pl.when(group < reducers)
    def _():
        total = sent_terms[0, :, pl.ds(pl.multiple_of(group * chunk, chunk), chunk)]
        for other in range(groups):
            scatter_copy(1, 0, other).wait_recv()
            total = total + met_terms[1, other]
        for other in range(groups):

            @pl.when(other != group)
            def _():
                scatter_copy(0, 0, other).wait_recv()

        for other in range(groups):
            total = total + jnp.where(other == group, 0.0, met_terms[0, other])
        final_terms[group] = total * (1.0 / groups)
        for other in range(groups):

            @pl.when(other != group)
            def _():
                gather_copy(group, other).start()

    for reducer in range(reducers):

        @pl.when(reducer != group)
        def _():
            gather_copy(reducer, 0).wait_recv()

        for slot in range(2):
            for row in range(3):
                sums_ref[0, row, slot : slot + 1, reducer * chunk : (reducer + 1) * chunk] = final_terms[
                    reducer, 3 * slot + row : 3 * slot + row + 1, :
                ]

    for other in range(groups):

        @pl.when((group < reducers) & (other != group))
        def _():
            gather_copy(group, other).wait_send()

    for reducer in range(reducers):
        scatter_copy(1, reducer, group).wait_send()

        @pl.when(reducer != group)
        def _():
            scatter_copy(0, reducer, group).wait_send()

    for d in range(2):
        ending = (chip == 0) if d == 0 else (chip == chips - 1)
        for m in range(2):
            out_copy(d, m).wait()

            @pl.when(core == 0)
            def _():
                for copy in operand_copies(d, m):
                    copy.wait_send()

            @pl.when(runner)
            def _():
                for at in range(3):
                    stage_copy(d, m, at).wait_send()

            @pl.when(runner & jnp.logical_not(ending))
            def _():
                for block in range(blocks):
                    hop(d, m, block).wait_send()


def body(
    section_of_layer, lengths, layer_gains, saved_queries, saved_keys, block_inputs, cotangents
):
    sections = lax.axis_size("section")
    groups = lax.axis_size("dp")
    seq, width = block_inputs.shape[3:]
    pairs = width // PAIR
    anywhere = pl.BlockSpec(memory_space=pl.ANY)
    scalars = pl.BlockSpec(memory_space=pltpu.SMEM)
    vector = pl.BlockSpec(memory_space=pltpu.VMEM)
    dma = pltpu.SemaphoreType.DMA
    reducers = 5
    row_blocks = 2
    input_grads, sums = pl.pallas_call(
        functools.partial(kernel, sections),
        out_shape=(
            jax.ShapeDtypeStruct(block_inputs.shape, BF16),
            jax.ShapeDtypeStruct((1, 3, 2, width), F32),
        ),
        in_specs=[scalars, scalars, anywhere, anywhere, anywhere, anywhere, anywhere],
        out_specs=(anywhere, vector),
        scratch_shapes=[
            pltpu.VMEM((3, layer_gains.shape[0], width), F32),
            pltpu.VMEM((2, 2, 8, width), F32),
            pltpu.VMEM((2, 8, width), F32),
            pltpu.VMEM((2, groups, 8, width // reducers), F32),
            pltpu.VMEM((reducers, 8, width // reducers), F32),
            pltpu.VMEM((2, 2, 2, seq, width), BF16),
            pltpu.VMEM((2, 2, 2, seq, width), BF16),
            pltpu.VMEM((2, 2, 2, seq, width), BF16),
            pltpu.VMEM((2, 2, 2, seq, width), BF16),
            pltpu.VMEM((2, 2, 2, seq, width), BF16),
            pltpu.VMEM((2, 2, 2, pairs, seq, 2 * seq), F32),
            pltpu.VMEM((2, 2, 2, 2, pairs, seq, 2 * seq), BF16),
            pltpu.VMEM((2, 2, 2, 2, seq, HEAD_DIM), F32),
            pltpu.VMEM((2, 2, 3, seq, width), BF16),
            pltpu.VMEM((2, 2, 2, seq, width), BF16),
            pltpu.VMEM((seq, width), F32),
            pltpu.VMEM((2, 2, 2, 8, width), F32),
            dma((2, 2, 5)),
            dma((2, 2)),
            dma((2, 2, 4)),
            dma((2, 2, 4)),
            dma((2, 2, row_blocks)),
            dma((2, 2, row_blocks)),
            dma((2, 2, 3)),
            dma((2, 2, 3)),
            dma((2, 2)),
            dma,
            dma((2, reducers)),
            dma((2, groups)),
            dma((groups,)),
            dma((reducers,)),
        ],
        compiler_params=pltpu.CompilerParams(
            collective_id=0, has_side_effects=True, vmem_limit_bytes=60000 * 1024
        ),
    )(
        section_of_layer,
        jnp.transpose(lengths, (0, 2, 1)),
        jnp.transpose(layer_gains, (1, 0, 2)),
        saved_queries,
        saved_keys,
        block_inputs,
        cotangents,
    )
    return (input_grads, jnp.transpose(sums, (0, 2, 1, 3)))


def solution(mesh):
    in_specs = (
        P(),
        P(None, None, "dp"),
        P(),
        P(None, "section", None, None, "dp", None),
        P(None, "section", None, None, "dp", None),
        P(None, "section", None, "dp", None),
        P(None, None, "dp", None),
    )
    out_specs = (P(None, "section", None, "dp", None), P("section", None, None, None))
    return jax.shard_map(body, mesh=mesh, in_specs=in_specs, out_specs=out_specs, check_vma=False)
```

```python
import functools
import math

import jax
import jax.numpy as jnp
from jax import lax
from jax.experimental import pallas as pl
from jax.experimental.pallas import tpu as pltpu
from jax.sharding import PartitionSpec as P

HEAD_DIM = 128
PAIR = 2 * HEAD_DIM
EPSILON = 1e-06
MESH = pl.DeviceIdType.MESH
F32 = jnp.float32
BF16 = jnp.bfloat16


def blocks_apart(pair):
    zero = jnp.zeros((pair.shape[0], HEAD_DIM), pair.dtype)
    upper = jnp.concatenate([pair[:, :HEAD_DIM], zero], axis=1)
    lower = jnp.concatenate([zero, pair[:, HEAD_DIM:]], axis=1)
    return jnp.concatenate([upper, lower], axis=0)


def dot(left, right, left_dim, right_dim):
    return lax.dot_general(
        left, right, (((left_dim,), (right_dim,)), ((), ())), preferred_element_type=F32
    )


def kernel(
    sections,
    layers_ref,
    lengths_ref,
    gains_hbm,
    queries_hbm,
    keys_hbm,
    inputs_hbm,
    cotangents_hbm,
    grads_hbm,
    sums_ref,
    gains_ref,
    terms_ref,
    sent_terms,
    met_terms,
    final_terms,
    q_buf,
    k_buf,
    h_low,
    h_high,
    v_buf,
    p_wide,
    p_low,
    r_buf,
    e_even,
    e_odd,
    x_buf,
    g_buf,
    load_sems,
    seed_sems,
    op_send,
    op_recv,
    hop_send,
    hop_recv,
    set_send,
    set_recv,
    out_sems,
    gain_sem,
    scatter_send,
    scatter_recv,
    gather_send,
    gather_recv,
):
    place = lax.axis_index("section")
    group = lax.axis_index("dp")
    groups = scatter_recv.shape[1]
    reducers = gather_recv.shape[0]
    core = lax.rem(place, 2)
    chip = lax.div(place, 2)
    chips = sections // 2
    seq = q_buf.shape[3]
    width = q_buf.shape[4]
    pairs = width // PAIR
    layer_total = layers_ref.shape[0]
    chunk = width // reducers
    blocks = hop_recv.shape[2]
    block_rows = seq // blocks
    scale = 1.0 / math.sqrt(HEAD_DIM)
    partner = {"section": place + 1 - 2 * core}
    first_direction = jnp.where(chip >= chips // 2, 0, 1)
    leads = (chip == chips - 1) | (chip == 0)

    def runner_of(d, at):
        middle = (at == chips // 2) | (at == chips // 2 - 1)
        later = jnp.where(at >= chips // 2, 1, 0)
        return jnp.where(middle & (d == later), 0, 1)

    def runs(d):
        return core == runner_of(d, chip)

    barrier = pltpu.get_barrier_semaphore()
    pl.semaphore_signal(barrier, inc=1, device_id=partner, device_id_type=MESH)
    neighbours = 2 * groups
    for d in range(2):
        for way in (-1, 1):
            at = chip + way
            linked = runs(d) & (at >= 0) & (at < chips)
            neighbours = neighbours + jnp.where(linked, 1, 0)

            @pl.when(linked)
            def _():
                pl.semaphore_signal(
                    barrier, inc=1, device_id={"section": 2 * at + runner_of(d, at)}, device_id_type=MESH
                )

    for other in range(groups):

        @pl.when(other != group)
        def _():
            pl.semaphore_signal(barrier, inc=1, device_id={"dp": jnp.int32(other)}, device_id_type=MESH)

        pl.semaphore_signal(
            barrier,
            inc=1,
            device_id={"section": sections - 1 - place, "dp": jnp.int32(other)},
            device_id_type=MESH,
        )

    gain_load = pltpu.make_async_copy(gains_hbm, gains_ref, gain_sem)
    gain_load.start()

    def state_load(d, m):
        return pltpu.make_async_copy(inputs_hbm.at[d, 0, m], h_low.at[d, m, 0], load_sems.at[d, m, 0])

    def head_loads(d, m, slot):
        return (
            pltpu.make_async_copy(
                keys_hbm.at[d, 0, slot, m], k_buf.at[d, m, slot], load_sems.at[d, m, 1 + 2 * slot]
            ),
            pltpu.make_async_copy(
                queries_hbm.at[d, 0, slot, m], q_buf.at[d, m, slot], load_sems.at[d, m, 2 + 2 * slot]
            ),
        )

    def seed(d, m):
        return pltpu.make_async_copy(cotangents_hbm.at[d, m], e_even.at[d, m, 0], seed_sems.at[d, m])

    for phase in range(2):
        d = first_direction if phase == 0 else 1 - first_direction
        for m in range(2):
            state_load(d, m).start()
            for slot in range(2):
                for copy in head_loads(d, m, slot):
                    copy.start()
            if phase == 0:

                @pl.when(leads & (core == 1))
                def _():
                    seed(d, m).start()

    gain_load.wait()

    for d in range(2):
        for whose in range(2):
            at = place if whose == 0 else place + 1 - 2 * core
            block = at if d == 0 else sections - 1 - at
            before = jnp.int32(0)
            for layer in range(layer_total):
                before = before + jnp.where(layers_ref[layer] < block, 1, 0)
            for slot in range(2):
                layer = jnp.minimum(before + slot, layer_total - 1)
                for row in range(3):
                    g_buf[d, whose, slot, row : row + 1, :] = gains_ref[row, pl.ds(layer, 1), :]

    terms_ref[...] = jnp.zeros_like(terms_ref)
    sent_terms[...] = jnp.zeros_like(sent_terms)
    met_terms[0, group] = jnp.zeros((8, chunk), F32)

    def second_layer(d):
        block = jnp.where(d == 0, place, sections - 1 - place)
        count = jnp.int32(0)
        for layer in range(layer_total):
            count = count + jnp.where(layers_ref[layer] == block, 1, 0)
        return count == 2

    def operand_copies(d, m):
        pieces = (
            (p_low.at[d, m, 0], p_low.at[d, m, 1]),
            (h_low.at[d, m, 0], h_low.at[d, m, 1]),
            (h_high.at[d, m, 0], h_high.at[d, m, 1]),
            (r_buf.at[d, m, 0], r_buf.at[d, m, 1]),
        )
        return [
            pltpu.make_async_remote_copy(
                src_ref=source,
                dst_ref=target,
                send_sem=op_send.at[d, m, at],
                recv_sem=op_recv.at[d, m, at],
                device_id=partner,
                device_id_type=MESH,
            )
            for at, (source, target) in enumerate(pieces)
        ]

    def hop(d, m, block):
        at = chip + jnp.where(d == 0, -1, 1)
        low = seq - (block + 1) * block_rows
        return pltpu.make_async_remote_copy(
            src_ref=e_even.at[d, m, 2, low : low + block_rows],
            dst_ref=e_even.at[d, m, 0, low : low + block_rows],
            send_sem=hop_send.at[d, m, block],
            recv_sem=hop_recv.at[d, m, block],
            device_id={"section": 2 * at + runner_of(d, at)},
            device_id_type=MESH,
        )

    def partner_visit(d):
        return jnp.where(core == 1, 1 - d, d)

    def stage_copy(d, m, at):
        visit = partner_visit(d)
        held = (e_even.at[d, m, visit], e_odd.at[d, m, visit], e_even.at[d, m, visit + 1])[at]
        met = (e_even.at[d, m, 0], e_odd.at[d, m, 0], e_even.at[d, m, 1])[at]
        return pltpu.make_async_remote_copy(
            src_ref=held,
            dst_ref=met,
            send_sem=set_send.at[d, m, at],
            recv_sem=set_recv.at[d, m, at],
            device_id=partner,
            device_id_type=MESH,
        )

    def own_base(d):
        return jnp.where(runs(d), 1 - partner_visit(d), 0)

    def out_copy(d, m):
        return pltpu.make_async_copy(e_even.at[d, m, own_base(d) + 1], grads_hbm.at[d, 0, m], out_sems.at[d, m])

    def lane_spread(column):
        return jnp.broadcast_to(column, (seq, HEAD_DIM))

    def prepare(d, m, t):
        two = second_layer(d)
        state_load(d, m).wait()
        length = lengths_ref[d, 0, m]
        key_at = lax.broadcasted_iota(jnp.int32, (seq, 2 * seq), 0)
        query_at = lax.rem(lax.broadcasted_iota(jnp.int32, (seq, 2 * seq), 1), seq)
        allowed = (key_at <= query_at) & (key_at < length)

        for slot in range(2):
            held = (h_low, h_high)[slot]
            for copy in head_loads(d, m, slot):
                copy.wait()
            squares = jnp.zeros((seq, HEAD_DIM), F32)
            for tile in range(width // HEAD_DIM):
                part = held[d, m, 0, :, tile * HEAD_DIM : (tile + 1) * HEAD_DIM].astype(F32)
                squares = squares + part * part
            inverse = lax.rsqrt(jnp.sum(squares, axis=1, keepdims=True) * (1.0 / width) + EPSILON)
            spread = lane_spread(inverse)
            spread_two = jnp.concatenate([spread, spread], axis=1)
            r_buf[d, m, 0, slot] = spread if slot == 0 else jnp.where(two, spread, 0.0)
            for pair in range(pairs):
                cols = slice(pair * PAIR, (pair + 1) * PAIR)
                state = held[d, m, 0, :, cols].astype(F32)
                values = (state * spread_two * g_buf[d, 0, slot, 0:1, cols]).astype(BF16)
                v_buf[d, m, slot, :, cols] = values
                scaled_q = (q_buf[d, m, slot, :, cols].astype(F32) * g_buf[d, 0, slot, 1:2, cols]).astype(BF16)
                scaled_k = (k_buf[d, m, slot, :, cols].astype(F32) * g_buf[d, 0, slot, 2:3, cols]).astype(BF16)
                scores = dot(scaled_k, blocks_apart(scaled_q), 1, 1) * scale
                masked = jnp.where(allowed, scores, -1e30)
                top = jnp.max(masked, axis=0, keepdims=True)
                terms = jnp.where(allowed, jnp.exp(masked - top), 0.0)
                probs = terms * (1.0 / jnp.sum(terms, axis=0, keepdims=True))
                low = probs.astype(BF16)
                p_wide[d, m, slot, pair] = probs
                p_low[d, m, 0, slot, pair] = low
                if slot == 0:
                    mixed = dot(low, values, 0, 0)
                    mixed = jnp.concatenate([mixed[:seq, :HEAD_DIM], mixed[seq:, HEAD_DIM:]], axis=1)
                    h_high[d, m, 0, :, cols] = (state + mixed).astype(BF16)

        @pl.when(t == 0)
        def _():
            pl.semaphore_wait(barrier, neighbours)

        @pl.when(jnp.logical_not(runs(d)))
        def _():
            for copy in operand_copies(d, m):
                copy.start()

    def chain_block(d, m, block, leading, ending):
        low = seq - (block + 1) * block_rows
        high = low + block_rows

        @pl.when(jnp.logical_not(leading))
        def _():
            hop(d, m, block).wait_recv()

        @pl.loop(0, 2)
        def _(visit):
            whose = jnp.where(visit == partner_visit(d), 1, 0)
            if block == 0:

                @pl.when(visit == partner_visit(d))
                def _():
                    for copy in operand_copies(d, m):
                        copy.wait_recv()

            for slot in (1, 0):
                if block == blocks - 1:
                    if slot == 1:

                        @pl.when(visit == partner_visit(d))
                        def _():
                            stage_copy(d, m, 0).start()

                        @pl.when(visit > partner_visit(d))
                        def _():
                            stage_copy(d, m, 2).start()

                    else:

                        @pl.when(visit == partner_visit(d))
                        def _():
                            stage_copy(d, m, 1).start()

                before, after = (e_odd, e_even) if slot == 0 else (e_even, e_odd)
                held = (h_low, h_high)[slot]
                onward = visit + 1 - slot
                total = jnp.zeros((block_rows, HEAD_DIM), F32)
                for pair in range(pairs):
                    cols = slice(pair * PAIR, (pair + 1) * PAIR)
                    grad = before[d, m, visit, low:seq, cols]
                    if low > 0:
                        grad = jnp.concatenate([jnp.zeros((low, PAIR), BF16), grad], axis=0)
                    product = dot(p_low[d, m, whose, slot, pair, low:high, :], blocks_apart(grad), 1, 0)
                    product = product * g_buf[d, whose, slot, 0:1, cols]
                    x_buf[low:high, cols] = product
                    weighed = product * held[d, m, whose, low:high, cols].astype(F32)
                    total = total + (weighed[:, :HEAD_DIM] + weighed[:, HEAD_DIM:])
                inverse = r_buf[d, m, whose, slot, low:high]
                shift = jnp.sum(total, axis=1, keepdims=True) * (1.0 / width)
                shift = jnp.broadcast_to(shift, (block_rows, HEAD_DIM)) * inverse * inverse * inverse
                for tile in range(width // HEAD_DIM):
                    cols = slice(tile * HEAD_DIM, (tile + 1) * HEAD_DIM)
                    state = held[d, m, whose, low:high, cols].astype(F32)
                    grad = before[d, m, visit, low:high, cols].astype(F32)
                    grad = grad + (inverse * x_buf[low:high, cols] - state * shift)
                    after[d, m, onward, low:high, cols] = grad.astype(BF16)

        @pl.when(jnp.logical_not(ending))
        def _():
            hop(d, m, block).start()

    def chain(d, m):
        leading = jnp.where(d == 0, chip == chips - 1, chip == 0)

        @pl.when(leading)
        def _():
            seed(d, m).wait()
            length = lengths_ref[d, 0, m]
            sequence_at = lax.broadcasted_iota(jnp.int32, (seq, PAIR), 0)
            for pair in range(pairs):
                cols = slice(pair * PAIR, (pair + 1) * PAIR)
                drawn = e_even[d, m, 0, :, cols].astype(F32)
                e_even[d, m, 0, :, cols] = jnp.where(sequence_at < length, drawn, 0.0).astype(BF16)

        ending = jnp.where(d == 0, chip == 0, chip == chips - 1)
        for block in range(blocks):
            chain_block(d, m, block, leading, ending)

        @pl.when(partner_visit(d) == 1)
        def _():
            stage_copy(d, m, 2).start()

    def gain_terms(d, m):
        two = second_layer(d)

        @pl.when(jnp.logical_not(runs(d)))
        def _():
            for at in range(3):
                stage_copy(d, m, at).wait_recv()

        out_copy(d, m).start()

        for slot in range(2):
            held = (h_low, h_high)[slot]
            stage = (e_odd, e_even)[slot]
            inverse = r_buf[d, m, 0, slot]
            inverse_two = jnp.concatenate([inverse, inverse], axis=1)
            for pair in range(pairs):
                cols = slice(pair * PAIR, (pair + 1) * PAIR)
                grad = blocks_apart(stage[d, m, own_base(d), :, cols])
                value_grad = dot(p_low[d, m, 0, slot, pair], grad, 1, 0)
                normed = held[d, m, 0, :, cols].astype(F32) * inverse_two
                norm_term = jnp.sum(value_grad * normed, axis=0, keepdims=True)
                probs_grad = dot(v_buf[d, m, slot, :, cols], grad, 1, 1)
                probs = p_wide[d, m, slot, pair]
                delta = jnp.sum(probs * probs_grad, axis=0, keepdims=True)
                score_grad = (probs * (probs_grad - delta) * scale).astype(BF16)
                met = dot(score_grad, blocks_apart(q_buf[d, m, slot, :, cols]), 1, 0)
                shared = jnp.sum(met * k_buf[d, m, slot, :, cols].astype(F32), axis=0, keepdims=True)
                shared = shared if slot == 0 else jnp.where(two, shared, 0.0)
                terms_ref[d, slot, 0:1, cols] += norm_term
                terms_ref[d, slot, 1:2, cols] += shared * g_buf[d, 0, slot, 2:3, cols]
                terms_ref[d, slot, 2:3, cols] += shared * g_buf[d, 0, slot, 1:2, cols]

    def scatter_copy(d, reducer, source):
        target = jnp.where(d == 0, place, sections - 1 - place)
        return pltpu.make_async_remote_copy(
            src_ref=sent_terms.at[d, :, reducer * chunk : (reducer + 1) * chunk],
            dst_ref=met_terms.at[d, source],
            send_sem=scatter_send.at[d, reducer],
            recv_sem=scatter_recv.at[d, source],
            device_id={"section": target, "dp": jnp.int32(reducer)},
            device_id_type=MESH,
        )

    def gather_copy(reducer, target):
        return pltpu.make_async_remote_copy(
            src_ref=final_terms.at[reducer],
            dst_ref=final_terms.at[reducer],
            send_sem=gather_send.at[target],
            recv_sem=gather_recv.at[reducer],
            device_id={"dp": jnp.int32(target)},
            device_id_type=MESH,
        )

    def scatter(d):
        for slot in range(2):
            for row in range(3):
                at = 3 * slot + row
                sent_terms[d, at : at + 1, :] = terms_ref[d, slot, row : row + 1, :]
        for reducer in range(reducers):

            @pl.when((d == 1) | (reducer != group))
            def _():
                scatter_copy(d, reducer, group).start()

    middle = (chip == chips // 2) | (chip == chips // 2 - 1)

    @pl.loop(0, 12)
    def _(t):
        odd = lax.rem(t, 2) == 1
        lead_unit = jnp.where(t < 4, lax.div(t, 2), jnp.where(t < 6, t - 2, jnp.where(t < 8, t - 6, lax.div(t - 4, 2))))
        other_unit = 2 * lax.div(t - 4, 4) + lax.rem(t - 4, 2)
        late_unit = jnp.where(middle, lax.rem(t, 4), other_unit)
        unit = jnp.where(leads, lead_unit, jnp.where(t < 4, t, late_unit))
        lead_chain = jnp.where(t < 4, odd, (t >= 8) & jnp.logical_not(odd))
        lead_terms = jnp.where(t < 8, t >= 6, odd)
        late_terms = jnp.where(middle, t >= 8, lax.rem(t, 4) >= 2)
        is_chain = jnp.where(leads, lead_chain, (t >= 4) & jnp.logical_not(late_terms))
        is_terms = jnp.where(leads, lead_terms, (t >= 4) & late_terms)
        d = jnp.where(unit < 2, first_direction, 1 - first_direction)
        m = lax.rem(unit, 2)

        @pl.when(jnp.logical_not(is_chain | is_terms))
        def _():
            prepare(d, m, t)

        @pl.when(is_chain & runs(d))
        def _():
            chain(d, m)

        @pl.when(is_terms)
        def _():
            gain_terms(d, m)

        @pl.when(is_terms & (m == 1))
        def _():
            scatter(d)

    @pl.when(group < reducers)
    def _():
        total = sent_terms[0, :, pl.ds(pl.multiple_of(group * chunk, chunk), chunk)]
        for other in range(groups):
            scatter_copy(1, 0, other).wait_recv()
            total = total + met_terms[1, other]
        for other in range(groups):

            @pl.when(other != group)
            def _():
                scatter_copy(0, 0, other).wait_recv()

        for other in range(groups):
            total = total + jnp.where(other == group, 0.0, met_terms[0, other])
        final_terms[group] = total * (1.0 / groups)
        for other in range(groups):

            @pl.when(other != group)
            def _():
                gather_copy(group, other).start()

    for reducer in range(reducers):

        @pl.when(reducer != group)
        def _():
            gather_copy(reducer, 0).wait_recv()

        for slot in range(2):
            for row in range(3):
                sums_ref[0, row, slot : slot + 1, reducer * chunk : (reducer + 1) * chunk] = final_terms[
                    reducer, 3 * slot + row : 3 * slot + row + 1, :
                ]

    for other in range(groups):

        @pl.when((group < reducers) & (other != group))
        def _():
            gather_copy(group, other).wait_send()

    for reducer in range(reducers):
        scatter_copy(1, reducer, group).wait_send()

        @pl.when(reducer != group)
        def _():
            scatter_copy(0, reducer, group).wait_send()

    for d in range(2):
        ending = (chip == 0) if d == 0 else (chip == chips - 1)
        for m in range(2):
            out_copy(d, m).wait()

            @pl.when(jnp.logical_not(runs(d)))
            def _():
                for copy in operand_copies(d, m):
                    copy.wait_send()

            @pl.when(runs(d))
            def _():
                for at in range(3):
                    stage_copy(d, m, at).wait_send()

            @pl.when(runs(d) & jnp.logical_not(ending))
            def _():
                for block in range(blocks):
                    hop(d, m, block).wait_send()


def body(
    section_of_layer, lengths, layer_gains, saved_queries, saved_keys, block_inputs, cotangents
):
    sections = lax.axis_size("section")
    groups = lax.axis_size("dp")
    seq, width = block_inputs.shape[3:]
    pairs = width // PAIR
    anywhere = pl.BlockSpec(memory_space=pl.ANY)
    scalars = pl.BlockSpec(memory_space=pltpu.SMEM)
    vector = pl.BlockSpec(memory_space=pltpu.VMEM)
    dma = pltpu.SemaphoreType.DMA
    reducers = 5
    row_blocks = 4
    input_grads, sums = pl.pallas_call(
        functools.partial(kernel, sections),
        out_shape=(
            jax.ShapeDtypeStruct(block_inputs.shape, BF16),
            jax.ShapeDtypeStruct((1, 3, 2, width), F32),
        ),
        in_specs=[scalars, scalars, anywhere, anywhere, anywhere, anywhere, anywhere],
        out_specs=(anywhere, vector),
        scratch_shapes=[
            pltpu.VMEM((3, layer_gains.shape[0], width), F32),
            pltpu.VMEM((2, 2, 8, width), F32),
            pltpu.VMEM((2, 8, width), F32),
            pltpu.VMEM((2, groups, 8, width // reducers), F32),
            pltpu.VMEM((reducers, 8, width // reducers), F32),
            pltpu.VMEM((2, 2, 2, seq, width), BF16),
            pltpu.VMEM((2, 2, 2, seq, width), BF16),
            pltpu.VMEM((2, 2, 2, seq, width), BF16),
            pltpu.VMEM((2, 2, 2, seq, width), BF16),
            pltpu.VMEM((2, 2, 2, seq, width), BF16),
            pltpu.VMEM((2, 2, 2, pairs, seq, 2 * seq), F32),
            pltpu.VMEM((2, 2, 2, 2, pairs, seq, 2 * seq), BF16),
            pltpu.VMEM((2, 2, 2, 2, seq, HEAD_DIM), F32),
            pltpu.VMEM((2, 2, 3, seq, width), BF16),
            pltpu.VMEM((2, 2, 2, seq, width), BF16),
            pltpu.VMEM((seq, width), F32),
            pltpu.VMEM((2, 2, 2, 8, width), F32),
            dma((2, 2, 5)),
            dma((2, 2)),
            dma((2, 2, 4)),
            dma((2, 2, 4)),
            dma((2, 2, row_blocks)),
            dma((2, 2, row_blocks)),
            dma((2, 2, 3)),
            dma((2, 2, 3)),
            dma((2, 2)),
            dma,
            dma((2, reducers)),
            dma((2, groups)),
            dma((groups,)),
            dma((reducers,)),
        ],
        compiler_params=pltpu.CompilerParams(
            collective_id=0, has_side_effects=True, vmem_limit_bytes=60000 * 1024
        ),
    )(
        section_of_layer,
        jnp.transpose(lengths, (0, 2, 1)),
        jnp.transpose(layer_gains, (1, 0, 2)),
        saved_queries,
        saved_keys,
        block_inputs,
        cotangents,
    )
    return (input_grads, jnp.transpose(sums, (0, 2, 1, 3)))


def solution(mesh):
    in_specs = (
        P(),
        P(None, None, "dp"),
        P(),
        P(None, "section", None, None, "dp", None),
        P(None, "section", None, None, "dp", None),
        P(None, "section", None, "dp", None),
        P(None, None, "dp", None),
    )
    out_specs = (P(None, "section", None, "dp", None), P("section", None, None, None))
    return jax.shard_map(body, mesh=mesh, in_specs=in_specs, out_specs=out_specs, check_vma=False)
```

```python
import functools
import math

import jax
import jax.numpy as jnp
from jax import lax
from jax.experimental import pallas as pl
from jax.experimental.pallas import tpu as pltpu
from jax.sharding import PartitionSpec as P

HEAD_DIM = 128
PAIR = 2 * HEAD_DIM
EPSILON = 1e-06
MESH = pl.DeviceIdType.MESH
F32 = jnp.float32
BF16 = jnp.bfloat16


def blocks_apart(pair):
    zero = jnp.zeros((pair.shape[0], HEAD_DIM), pair.dtype)
    upper = jnp.concatenate([pair[:, :HEAD_DIM], zero], axis=1)
    lower = jnp.concatenate([zero, pair[:, HEAD_DIM:]], axis=1)
    return jnp.concatenate([upper, lower], axis=0)


def dot(left, right, left_dim, right_dim):
    return lax.dot_general(
        left, right, (((left_dim,), (right_dim,)), ((), ())), preferred_element_type=F32
    )


def kernel(
    sections,
    layers_ref,
    lengths_ref,
    gains_hbm,
    queries_hbm,
    keys_hbm,
    inputs_hbm,
    cotangents_hbm,
    grads_hbm,
    sums_ref,
    gains_ref,
    terms_ref,
    sent_terms,
    met_terms,
    final_terms,
    q_buf,
    k_buf,
    h_low,
    h_high,
    v_buf,
    p_wide,
    p_low,
    r_buf,
    e_even,
    e_odd,
    x_buf,
    g_buf,
    load_sems,
    seed_sems,
    op_send,
    op_recv,
    hop_send,
    hop_recv,
    set_send,
    set_recv,
    out_sems,
    gain_sem,
    scatter_send,
    scatter_recv,
    gather_send,
    gather_recv,
):
    place = lax.axis_index("section")
    group = lax.axis_index("dp")
    groups = scatter_recv.shape[1]
    reducers = gather_recv.shape[0]
    core = lax.rem(place, 2)
    chip = lax.div(place, 2)
    chips = sections // 2
    seq = q_buf.shape[3]
    width = q_buf.shape[4]
    pairs = width // PAIR
    layer_total = layers_ref.shape[0]
    chunk = width // reducers
    blocks = hop_recv.shape[2]
    block_rows = seq // blocks
    scale = 1.0 / math.sqrt(HEAD_DIM)
    partner = {"section": place + 1 - 2 * core}
    first_direction = jnp.where(chip >= chips // 2, 0, 1)
    leads = (chip == chips - 1) | (chip == 0)

    def runner_of(d, at):
        middle = (at == chips // 2) | (at == chips // 2 - 1)
        later = jnp.where(at >= chips // 2, 1, 0)
        return jnp.where(middle & (d == later), 0, 1)

    def runs(d):
        return core == runner_of(d, chip)

    barrier = pltpu.get_barrier_semaphore()
    pl.semaphore_signal(barrier, inc=1, device_id=partner, device_id_type=MESH)
    neighbours = 2 * groups
    for d in range(2):
        for way in (-1, 1):
            at = chip + way
            linked = runs(d) & (at >= 0) & (at < chips)
            neighbours = neighbours + jnp.where(linked, 1, 0)

            @pl.when(linked)
            def _():
                pl.semaphore_signal(
                    barrier, inc=1, device_id={"section": 2 * at + runner_of(d, at)}, device_id_type=MESH
                )

    for other in range(groups):

        @pl.when(other != group)
        def _():
            pl.semaphore_signal(barrier, inc=1, device_id={"dp": jnp.int32(other)}, device_id_type=MESH)

        pl.semaphore_signal(
            barrier,
            inc=1,
            device_id={"section": sections - 1 - place, "dp": jnp.int32(other)},
            device_id_type=MESH,
        )

    gain_load = pltpu.make_async_copy(gains_hbm, gains_ref, gain_sem)
    gain_load.start()

    def state_load(d, m):
        return pltpu.make_async_copy(inputs_hbm.at[d, 0, m], h_low.at[d, m, 0], load_sems.at[d, m, 0])

    def head_loads(d, m, slot):
        return (
            pltpu.make_async_copy(
                keys_hbm.at[d, 0, slot, m], k_buf.at[d, m, slot], load_sems.at[d, m, 1 + 2 * slot]
            ),
            pltpu.make_async_copy(
                queries_hbm.at[d, 0, slot, m], q_buf.at[d, m, slot], load_sems.at[d, m, 2 + 2 * slot]
            ),
        )

    def seed(d, m):
        return pltpu.make_async_copy(cotangents_hbm.at[d, m], e_even.at[d, m, 0], seed_sems.at[d, m])

    for phase in range(2):
        d = first_direction if phase == 0 else 1 - first_direction
        for m in range(2):
            state_load(d, m).start()
            for slot in range(2):
                for copy in head_loads(d, m, slot):
                    copy.start()
            if phase == 0:

                @pl.when(leads & (core == 1))
                def _():
                    seed(d, m).start()

    gain_load.wait()

    for d in range(2):
        for whose in range(2):
            at = place if whose == 0 else place + 1 - 2 * core
            block = at if d == 0 else sections - 1 - at
            before = jnp.int32(0)
            for layer in range(layer_total):
                before = before + jnp.where(layers_ref[layer] < block, 1, 0)
            for slot in range(2):
                layer = jnp.minimum(before + slot, layer_total - 1)
                for row in range(3):
                    g_buf[d, whose, slot, row : row + 1, :] = gains_ref[row, pl.ds(layer, 1), :]

    terms_ref[...] = jnp.zeros_like(terms_ref)
    sent_terms[...] = jnp.zeros_like(sent_terms)
    met_terms[0, group] = jnp.zeros((8, chunk), F32)

    def second_layer(d):
        block = jnp.where(d == 0, place, sections - 1 - place)
        count = jnp.int32(0)
        for layer in range(layer_total):
            count = count + jnp.where(layers_ref[layer] == block, 1, 0)
        return count == 2

    def operand_copies(d, m):
        pieces = (
            (p_low.at[d, m, 0, 1], p_low.at[d, m, 1, 1]),
            (h_high.at[d, m, 0], h_high.at[d, m, 1]),
            (r_buf.at[d, m, 0], r_buf.at[d, m, 1]),
            (p_low.at[d, m, 0, 0], p_low.at[d, m, 1, 0]),
            (h_low.at[d, m, 0], h_low.at[d, m, 1]),
        )
        return [
            pltpu.make_async_remote_copy(
                src_ref=source,
                dst_ref=target,
                send_sem=op_send.at[d, m, at],
                recv_sem=op_recv.at[d, m, at],
                device_id=partner,
                device_id_type=MESH,
            )
            for at, (source, target) in enumerate(pieces)
        ]

    def hop(d, m, block):
        at = chip + jnp.where(d == 0, -1, 1)
        low = seq - (block + 1) * block_rows
        return pltpu.make_async_remote_copy(
            src_ref=e_even.at[d, m, 2, low : low + block_rows],
            dst_ref=e_even.at[d, m, 0, low : low + block_rows],
            send_sem=hop_send.at[d, m, block],
            recv_sem=hop_recv.at[d, m, block],
            device_id={"section": 2 * at + runner_of(d, at)},
            device_id_type=MESH,
        )

    def partner_visit(d):
        return jnp.where(core == 1, 1 - d, d)

    def stage_copy(d, m, at):
        visit = partner_visit(d)
        held = (e_even.at[d, m, visit], e_odd.at[d, m, visit], e_even.at[d, m, visit + 1])[at]
        met = (e_even.at[d, m, 0], e_odd.at[d, m, 0], e_even.at[d, m, 1])[at]
        return pltpu.make_async_remote_copy(
            src_ref=held,
            dst_ref=met,
            send_sem=set_send.at[d, m, at],
            recv_sem=set_recv.at[d, m, at],
            device_id=partner,
            device_id_type=MESH,
        )

    def own_base(d):
        return jnp.where(runs(d), 1 - partner_visit(d), 0)

    def out_copy(d, m):
        return pltpu.make_async_copy(e_even.at[d, m, own_base(d) + 1], grads_hbm.at[d, 0, m], out_sems.at[d, m])

    def lane_spread(column):
        return jnp.broadcast_to(column, (seq, HEAD_DIM))

    def prepare(d, m, t):
        two = second_layer(d)
        state_load(d, m).wait()
        length = lengths_ref[d, 0, m]
        key_at = lax.broadcasted_iota(jnp.int32, (seq, 2 * seq), 0)
        query_at = lax.rem(lax.broadcasted_iota(jnp.int32, (seq, 2 * seq), 1), seq)
        allowed = (key_at <= query_at) & (key_at < length)

        for slot in range(2):
            held = (h_low, h_high)[slot]
            for copy in head_loads(d, m, slot):
                copy.wait()
            squares = jnp.zeros((seq, HEAD_DIM), F32)
            for tile in range(width // HEAD_DIM):
                part = held[d, m, 0, :, tile * HEAD_DIM : (tile + 1) * HEAD_DIM].astype(F32)
                squares = squares + part * part
            inverse = lax.rsqrt(jnp.sum(squares, axis=1, keepdims=True) * (1.0 / width) + EPSILON)
            spread = lane_spread(inverse)
            spread_two = jnp.concatenate([spread, spread], axis=1)
            r_buf[d, m, 0, slot] = spread if slot == 0 else jnp.where(two, spread, 0.0)
            for pair in range(pairs):
                cols = slice(pair * PAIR, (pair + 1) * PAIR)
                state = held[d, m, 0, :, cols].astype(F32)
                values = (state * spread_two * g_buf[d, 0, slot, 0:1, cols]).astype(BF16)
                v_buf[d, m, slot, :, cols] = values
                scaled_q = (q_buf[d, m, slot, :, cols].astype(F32) * g_buf[d, 0, slot, 1:2, cols]).astype(BF16)
                scaled_k = (k_buf[d, m, slot, :, cols].astype(F32) * g_buf[d, 0, slot, 2:3, cols]).astype(BF16)
                scores = dot(scaled_k, blocks_apart(scaled_q), 1, 1) * scale
                masked = jnp.where(allowed, scores, -1e30)
                top = jnp.max(masked, axis=0, keepdims=True)
                terms = jnp.where(allowed, jnp.exp(masked - top), 0.0)
                probs = terms * (1.0 / jnp.sum(terms, axis=0, keepdims=True))
                low = probs.astype(BF16)
                p_wide[d, m, slot, pair] = probs
                p_low[d, m, 0, slot, pair] = low
                if slot == 0:
                    mixed = dot(low, values, 0, 0)
                    mixed = jnp.concatenate([mixed[:seq, :HEAD_DIM], mixed[seq:, HEAD_DIM:]], axis=1)
                    h_high[d, m, 0, :, cols] = (state + mixed).astype(BF16)

        @pl.when(t == 0)
        def _():
            pl.semaphore_wait(barrier, neighbours)

        @pl.when(jnp.logical_not(runs(d)))
        def _():
            for copy in operand_copies(d, m):
                copy.start()

    def chain_block(d, m, block, leading, ending):
        low = seq - (block + 1) * block_rows
        high = low + block_rows

        @pl.when(jnp.logical_not(leading))
        def _():
            hop(d, m, block).wait_recv()

        @pl.loop(0, 2)
        def _(visit):
            whose = jnp.where(visit == partner_visit(d), 1, 0)
            for slot in (1, 0):
                if block == 0:

                    @pl.when(visit == partner_visit(d))
                    def _():
                        for copy in operand_copies(d, m)[3 - 3 * slot : 5 - 2 * slot]:
                            copy.wait_recv()

                if block == blocks - 1:
                    if slot == 1:

                        @pl.when(visit == partner_visit(d))
                        def _():
                            stage_copy(d, m, 0).start()

                        @pl.when(visit > partner_visit(d))
                        def _():
                            stage_copy(d, m, 2).start()

                    else:

                        @pl.when(visit == partner_visit(d))
                        def _():
                            stage_copy(d, m, 1).start()

                before, after = (e_odd, e_even) if slot == 0 else (e_even, e_odd)
                held = (h_low, h_high)[slot]
                onward = visit + 1 - slot
                total = jnp.zeros((block_rows, HEAD_DIM), F32)
                for pair in range(pairs):
                    cols = slice(pair * PAIR, (pair + 1) * PAIR)
                    grad = before[d, m, visit, low:seq, cols]
                    if low > 0:
                        grad = jnp.concatenate([jnp.zeros((low, PAIR), BF16), grad], axis=0)
                    product = dot(p_low[d, m, whose, slot, pair, low:high, :], blocks_apart(grad), 1, 0)
                    product = product * g_buf[d, whose, slot, 0:1, cols]
                    x_buf[low:high, cols] = product
                    weighed = product * held[d, m, whose, low:high, cols].astype(F32)
                    total = total + (weighed[:, :HEAD_DIM] + weighed[:, HEAD_DIM:])
                inverse = r_buf[d, m, whose, slot, low:high]
                shift = jnp.sum(total, axis=1, keepdims=True) * (1.0 / width)
                shift = jnp.broadcast_to(shift, (block_rows, HEAD_DIM)) * inverse * inverse * inverse
                for tile in range(width // HEAD_DIM):
                    cols = slice(tile * HEAD_DIM, (tile + 1) * HEAD_DIM)
                    state = held[d, m, whose, low:high, cols].astype(F32)
                    grad = before[d, m, visit, low:high, cols].astype(F32)
                    grad = grad + (inverse * x_buf[low:high, cols] - state * shift)
                    after[d, m, onward, low:high, cols] = grad.astype(BF16)

        @pl.when(jnp.logical_not(ending))
        def _():
            hop(d, m, block).start()

    def chain(d, m):
        leading = jnp.where(d == 0, chip == chips - 1, chip == 0)

        @pl.when(leading)
        def _():
            seed(d, m).wait()
            length = lengths_ref[d, 0, m]
            sequence_at = lax.broadcasted_iota(jnp.int32, (seq, PAIR), 0)
            for pair in range(pairs):
                cols = slice(pair * PAIR, (pair + 1) * PAIR)
                drawn = e_even[d, m, 0, :, cols].astype(F32)
                e_even[d, m, 0, :, cols] = jnp.where(sequence_at < length, drawn, 0.0).astype(BF16)

        ending = jnp.where(d == 0, chip == 0, chip == chips - 1)
        for block in range(blocks):
            chain_block(d, m, block, leading, ending)

        @pl.when(partner_visit(d) == 1)
        def _():
            stage_copy(d, m, 2).start()

    def gain_terms(d, m):
        two = second_layer(d)

        @pl.when(jnp.logical_not(runs(d)))
        def _():
            for at in range(3):
                stage_copy(d, m, at).wait_recv()

        out_copy(d, m).start()

        for slot in range(2):
            held = (h_low, h_high)[slot]
            stage = (e_odd, e_even)[slot]
            inverse = r_buf[d, m, 0, slot]
            inverse_two = jnp.concatenate([inverse, inverse], axis=1)
            for pair in range(pairs):
                cols = slice(pair * PAIR, (pair + 1) * PAIR)
                grad = blocks_apart(stage[d, m, own_base(d), :, cols])
                value_grad = dot(p_low[d, m, 0, slot, pair], grad, 1, 0)
                normed = held[d, m, 0, :, cols].astype(F32) * inverse_two
                norm_term = jnp.sum(value_grad * normed, axis=0, keepdims=True)
                probs_grad = dot(v_buf[d, m, slot, :, cols], grad, 1, 1)
                probs = p_wide[d, m, slot, pair]
                delta = jnp.sum(probs * probs_grad, axis=0, keepdims=True)
                score_grad = (probs * (probs_grad - delta) * scale).astype(BF16)
                met = dot(score_grad, blocks_apart(q_buf[d, m, slot, :, cols]), 1, 0)
                shared = jnp.sum(met * k_buf[d, m, slot, :, cols].astype(F32), axis=0, keepdims=True)
                shared = shared if slot == 0 else jnp.where(two, shared, 0.0)
                terms_ref[d, slot, 0:1, cols] += norm_term
                terms_ref[d, slot, 1:2, cols] += shared * g_buf[d, 0, slot, 2:3, cols]
                terms_ref[d, slot, 2:3, cols] += shared * g_buf[d, 0, slot, 1:2, cols]

    def scatter_copy(d, reducer, source):
        target = jnp.where(d == 0, place, sections - 1 - place)
        return pltpu.make_async_remote_copy(
            src_ref=sent_terms.at[d, :, reducer * chunk : (reducer + 1) * chunk],
            dst_ref=met_terms.at[d, source],
            send_sem=scatter_send.at[d, reducer],
            recv_sem=scatter_recv.at[d, source],
            device_id={"section": target, "dp": jnp.int32(reducer)},
            device_id_type=MESH,
        )

    def gather_copy(reducer, target):
        return pltpu.make_async_remote_copy(
            src_ref=final_terms.at[reducer],
            dst_ref=final_terms.at[reducer],
            send_sem=gather_send.at[target],
            recv_sem=gather_recv.at[reducer],
            device_id={"dp": jnp.int32(target)},
            device_id_type=MESH,
        )

    def scatter(d):
        for slot in range(2):
            for row in range(3):
                at = 3 * slot + row
                sent_terms[d, at : at + 1, :] = terms_ref[d, slot, row : row + 1, :]
        for reducer in range(reducers):

            @pl.when((d == 1) | (reducer != group))
            def _():
                scatter_copy(d, reducer, group).start()

    inner = (chip >= chips // 2 - 2) & (chip <= chips // 2 + 1)

    @pl.loop(0, 12)
    def _(t):
        odd = lax.rem(t, 2) == 1
        lead_unit = jnp.where(t < 4, lax.div(t, 2), jnp.where(t < 6, t - 2, jnp.where(t < 8, t - 6, lax.div(t - 4, 2))))
        other_unit = 2 * lax.div(t - 4, 4) + lax.rem(t - 4, 2)
        late_unit = jnp.where(inner, lax.rem(t, 4), other_unit)
        unit = jnp.where(leads, lead_unit, jnp.where(t < 4, t, late_unit))
        lead_chain = jnp.where(t < 4, odd, (t >= 8) & jnp.logical_not(odd))
        lead_terms = jnp.where(t < 8, t >= 6, odd)
        late_terms = jnp.where(inner, t >= 8, lax.rem(t, 4) >= 2)
        is_chain = jnp.where(leads, lead_chain, (t >= 4) & jnp.logical_not(late_terms))
        is_terms = jnp.where(leads, lead_terms, (t >= 4) & late_terms)
        d = jnp.where(unit < 2, first_direction, 1 - first_direction)
        m = lax.rem(unit, 2)

        @pl.when(jnp.logical_not(is_chain | is_terms))
        def _():
            prepare(d, m, t)

        @pl.when(is_chain & runs(d))
        def _():
            chain(d, m)

        @pl.when(is_terms)
        def _():
            gain_terms(d, m)

        @pl.when(is_terms & (m == 1))
        def _():
            scatter(d)

    @pl.when(group < reducers)
    def _():
        total = sent_terms[0, :, pl.ds(pl.multiple_of(group * chunk, chunk), chunk)]
        for other in range(groups):
            scatter_copy(1, 0, other).wait_recv()
            total = total + met_terms[1, other]
        for other in range(groups):

            @pl.when(other != group)
            def _():
                scatter_copy(0, 0, other).wait_recv()

        for other in range(groups):
            total = total + jnp.where(other == group, 0.0, met_terms[0, other])
        final_terms[group] = total * (1.0 / groups)
        for other in range(groups):

            @pl.when(other != group)
            def _():
                gather_copy(group, other).start()

    for reducer in range(reducers):

        @pl.when(reducer != group)
        def _():
            gather_copy(reducer, 0).wait_recv()

        for slot in range(2):
            for row in range(3):
                sums_ref[0, row, slot : slot + 1, reducer * chunk : (reducer + 1) * chunk] = final_terms[
                    reducer, 3 * slot + row : 3 * slot + row + 1, :
                ]

    for other in range(groups):

        @pl.when((group < reducers) & (other != group))
        def _():
            gather_copy(group, other).wait_send()

    for reducer in range(reducers):
        scatter_copy(1, reducer, group).wait_send()

        @pl.when(reducer != group)
        def _():
            scatter_copy(0, reducer, group).wait_send()

    for d in range(2):
        ending = (chip == 0) if d == 0 else (chip == chips - 1)
        for m in range(2):
            out_copy(d, m).wait()

            @pl.when(jnp.logical_not(runs(d)))
            def _():
                for copy in operand_copies(d, m):
                    copy.wait_send()

            @pl.when(runs(d))
            def _():
                for at in range(3):
                    stage_copy(d, m, at).wait_send()

            @pl.when(runs(d) & jnp.logical_not(ending))
            def _():
                for block in range(blocks):
                    hop(d, m, block).wait_send()


def body(
    section_of_layer, lengths, layer_gains, saved_queries, saved_keys, block_inputs, cotangents
):
    sections = lax.axis_size("section")
    groups = lax.axis_size("dp")
    seq, width = block_inputs.shape[3:]
    pairs = width // PAIR
    anywhere = pl.BlockSpec(memory_space=pl.ANY)
    scalars = pl.BlockSpec(memory_space=pltpu.SMEM)
    vector = pl.BlockSpec(memory_space=pltpu.VMEM)
    dma = pltpu.SemaphoreType.DMA
    reducers = 5
    row_blocks = 4
    input_grads, sums = pl.pallas_call(
        functools.partial(kernel, sections),
        out_shape=(
            jax.ShapeDtypeStruct(block_inputs.shape, BF16),
            jax.ShapeDtypeStruct((1, 3, 2, width), F32),
        ),
        in_specs=[scalars, scalars, anywhere, anywhere, anywhere, anywhere, anywhere],
        out_specs=(anywhere, vector),
        scratch_shapes=[
            pltpu.VMEM((3, layer_gains.shape[0], width), F32),
            pltpu.VMEM((2, 2, 8, width), F32),
            pltpu.VMEM((2, 8, width), F32),
            pltpu.VMEM((2, groups, 8, width // reducers), F32),
            pltpu.VMEM((reducers, 8, width // reducers), F32),
            pltpu.VMEM((2, 2, 2, seq, width), BF16),
            pltpu.VMEM((2, 2, 2, seq, width), BF16),
            pltpu.VMEM((2, 2, 2, seq, width), BF16),
            pltpu.VMEM((2, 2, 2, seq, width), BF16),
            pltpu.VMEM((2, 2, 2, seq, width), BF16),
            pltpu.VMEM((2, 2, 2, pairs, seq, 2 * seq), F32),
            pltpu.VMEM((2, 2, 2, 2, pairs, seq, 2 * seq), BF16),
            pltpu.VMEM((2, 2, 2, 2, seq, HEAD_DIM), F32),
            pltpu.VMEM((2, 2, 3, seq, width), BF16),
            pltpu.VMEM((2, 2, 2, seq, width), BF16),
            pltpu.VMEM((seq, width), F32),
            pltpu.VMEM((2, 2, 2, 8, width), F32),
            dma((2, 2, 5)),
            dma((2, 2)),
            dma((2, 2, 5)),
            dma((2, 2, 5)),
            dma((2, 2, row_blocks)),
            dma((2, 2, row_blocks)),
            dma((2, 2, 3)),
            dma((2, 2, 3)),
            dma((2, 2)),
            dma,
            dma((2, reducers)),
            dma((2, groups)),
            dma((groups,)),
            dma((reducers,)),
        ],
        compiler_params=pltpu.CompilerParams(
            collective_id=0, has_side_effects=True, vmem_limit_bytes=60000 * 1024
        ),
    )(
        section_of_layer,
        jnp.transpose(lengths, (0, 2, 1)),
        jnp.transpose(layer_gains, (1, 0, 2)),
        saved_queries,
        saved_keys,
        block_inputs,
        cotangents,
    )
    return (input_grads, jnp.transpose(sums, (0, 2, 1, 3)))


def solution(mesh):
    in_specs = (
        P(),
        P(None, None, "dp"),
        P(),
        P(None, "section", None, None, "dp", None),
        P(None, "section", None, None, "dp", None),
        P(None, "section", None, "dp", None),
        P(None, None, "dp", None),
    )
    out_specs = (P(None, "section", None, "dp", None), P("section", None, None, None))
    return jax.shard_map(body, mesh=mesh, in_specs=in_specs, out_specs=out_specs, check_vma=False)
```
